32 devices in a mesh: dp: 2 (over x), tm: 4 (over z), space: 4 (over y, core).
Axes of the slice: x: 2, y: 2, z: 4, core: 2. Of those that a mesh axis runs over, the one named last changes fastest.
Arguments:
- latent: bfloat16 [2, 12, 8, 104, 384], P('dp', 'tm', 'space'), may hold values from -16 to 16
- attn_gain: float32 [384], replicated, may hold values from 0.5 to 1.5
- w_query: bfloat16 [384, 384], replicated, may hold values from -1 to 1
- w_key: bfloat16 [384, 384], replicated, may hold values from -1 to 1
- w_value: bfloat16 [384, 384], replicated, may hold values from -0.3125 to 0.3125
- w_out: bfloat16 [384, 384], replicated, may hold values from -1.25 to 1.25
- conv_gain_first: float32 [384], replicated, may hold values from 0.5 to 1.5
- conv_first: bfloat16 [3, 3, 3, 384, 384], replicated, may hold values from -0.0625 to 0.0625
- conv_gain_second: float32 [384], replicated, may hold values from 0.5 to 1.5
- conv_second: bfloat16 [3, 3, 3, 384, 384], replicated, may hold values from -0.0625 to 0.0625
- student_in: bfloat16 [384, 384], replicated, may hold values from -0.3125 to 0.3125
- student_out: bfloat16 [384, 384], replicated, may hold values from -0.3125 to 0.3125
Outputs:
- teacher_out: bfloat16 [2, 12, 8, 104, 384], P('dp', 'tm', 'space')
- grad_in: float32 [384, 384], replicated
- grad_out: float32 [384, 384], replicated
The draws below stay inside these ranges and needn't reach their ends.
All inputs are finite; a program needn't handle non-finite values.
Results may differ from the reference program's by a relative error of at most 0.007.
Values may be sent and summed in bfloat16 or wider, within the bound.
No kernel may reach another device: no remote copies, remote signals or barrier semaphores. Data moves between devices by JAX's collectives and lax.ppermute only.
A program may use at most 128 MiB of HBM per device.

```python
import math
import jax
import jax.numpy as jnp
from jax import lax

C = 384
WIDTH = 104
CLIPS = 2
FRAMES = 12
ROWS = 8
TOKENS = 19968


def draw_latent(key, part):
    shape = (CLIPS, FRAMES, ROWS, WIDTH, C)
    drawn = jax.random.normal(jax.random.fold_in(key, 1), shape, jnp.float32)
    result = jnp.clip(drawn, -6.0, 6.0)
    return result.astype(jnp.bfloat16)


def projection_draw(key, salt):
    gaussian = jax.random.normal(jax.random.fold_in(key, salt), (C, C), jnp.float32)
    matrix = gaussian * math.sqrt(2.0 / C)
    return jnp.clip(matrix, -1.0, 1.0).astype(jnp.bfloat16)


def draw_w_query(key, part):
    return projection_draw(key, 11)


def draw_w_key(key, part):
    return projection_draw(key, 12)


def bell_draw(rng, dims, width, bound, held_as=jnp.bfloat16):
    return jnp.clip(width * jax.random.normal(rng, dims, jnp.float32), -bound, bound).astype(held_as)


def setup_inputs(seed: int = 0) -> dict:
    keys = jax.random.split(jax.random.key(seed), 13)
    return {
        "latent": draw_latent(jax.random.fold_in(keys[12], 71), 0),
        "attn_gain": jnp.clip(1.0 + 0.1 * jax.random.normal(keys[1], (C,), jnp.float32), 0.5, 1.5),
        "w_query": draw_w_query(jax.random.fold_in(keys[12], 71), 0),
        "w_key": draw_w_key(jax.random.fold_in(keys[12], 71), 0),
        "w_value": bell_draw(keys[4], (C, C), C ** -0.5, 0.3125),
        "w_out": bell_draw(keys[5], (C, C), (C // 16) ** -0.5, 1.25),
        "conv_gain_first": jnp.clip(1.0 + 0.1 * jax.random.normal(keys[6], (C,), jnp.float32), 0.5, 1.5),
        "conv_first": bell_draw(keys[7], (3, 3, 3, C, C), (27 * C) ** -0.5, 0.0625),
        "conv_gain_second": jnp.clip(1.0 + 0.1 * jax.random.normal(keys[8], (C,), jnp.float32), 0.5, 1.5),
        "conv_second": bell_draw(keys[9], (3, 3, 3, C, C), (27 * C) ** -0.5, 0.0625),
        "student_in": bell_draw(keys[10], (C, C), C ** -0.5, 0.3125),
        "student_out": bell_draw(keys[11], (C, C), C ** -0.5, 0.3125),
    }


def root_norm(values, gain):
    return values * lax.rsqrt(lax.optimization_barrier(jnp.mean(values * values, axis=-1, keepdims=True)) + 1e-06) * gain

def causal_conv(activation, weight):
    padded = jnp.pad(activation, ((0, 0), (2, 0), (1, 1), (1, 1), (0, 0)))
    total = jnp.zeros((CLIPS * FRAMES * ROWS * WIDTH, C), jnp.float32)
    for tap_time in range(3):
        for tap_row in range(3):
            for tap_col in range(3):
                window = padded[:, tap_time:tap_time + FRAMES, tap_row:tap_row + ROWS, tap_col:tap_col + WIDTH]
                total = total + jnp.dot(window.reshape(-1, C), weight[tap_time, tap_row, tap_col], preferred_element_type=jnp.float32)
    return total

def reference(latent, attn_gain, w_query, w_key, w_value, w_out, conv_gain_first, conv_first, conv_gain_second, conv_second, student_in, student_out):
    flat = latent.reshape(-1, C)
    inputs_wide = flat.astype(jnp.float32)
    normed = root_norm(inputs_wide, attn_gain).astype(jnp.bfloat16)
    queries = jnp.dot(normed, w_query, preferred_element_type=jnp.float32).astype(jnp.bfloat16)
    keys_all = jnp.dot(normed, w_key, preferred_element_type=jnp.float32).astype(jnp.bfloat16)
    values_all = jnp.dot(normed, w_value, preferred_element_type=jnp.float32).astype(jnp.bfloat16)
    per_frame = ROWS * WIDTH
    frame_total = CLIPS * FRAMES
    scale = C ** (-0.5)

    def one_frame(block):
        frame_queries, frame_keys, frame_values = block
        scores = jnp.dot(frame_queries, frame_keys.T, preferred_element_type=jnp.float32) * scale
        maxima = lax.optimization_barrier(jnp.max(scores, axis=-1, keepdims=True))
        expos = jnp.exp(scores - maxima)
        totals = lax.optimization_barrier(jnp.sum(expos, axis=-1, keepdims=True))
        weights = expos.astype(jnp.bfloat16)
        summed = jnp.dot(weights, frame_values, preferred_element_type=jnp.float32)
        return (summed / totals).astype(jnp.bfloat16)
    mixed = lax.map(one_frame, (queries.reshape(frame_total, per_frame, C), keys_all.reshape(frame_total, per_frame, C), values_all.reshape(frame_total, per_frame, C)))
    mixed = mixed.reshape(-1, C)
    mid = (inputs_wide + jnp.dot(mixed, w_out, preferred_element_type=jnp.float32)).astype(jnp.bfloat16)
    mid_wide = mid.astype(jnp.float32)
    first_act = jax.nn.silu(root_norm(mid_wide, conv_gain_first)).astype(jnp.bfloat16)
    first_conv = causal_conv(first_act.reshape(CLIPS, FRAMES, ROWS, WIDTH, C), conv_first)
    second_act = jax.nn.silu(root_norm(first_conv, conv_gain_second)).astype(jnp.bfloat16)
    second_conv = causal_conv(second_act.reshape(CLIPS, FRAMES, ROWS, WIDTH, C), conv_second)
    teacher = (mid_wide + second_conv).astype(jnp.bfloat16)
    student_pre = jnp.dot(flat, student_in, preferred_element_type=jnp.float32)
    student_hidden = jax.nn.silu(student_pre).astype(jnp.bfloat16)
    predicted = inputs_wide + jnp.dot(student_hidden, student_out, preferred_element_type=jnp.float32)
    error = predicted - teacher.astype(jnp.float32)
    signal = (error * lax.rsqrt(error * error + 0.0625) * TOKENS ** (-0.5)).astype(jnp.bfloat16)
    over_tokens = (((0,), (0,)), ((), ()))
    grad_out = lax.dot_general(student_hidden, signal, over_tokens, preferred_element_type=jnp.float32)
    back = lax.dot_general(signal, student_out, (((1,), (1,)), ((), ())), preferred_element_type=jnp.float32)
    logistic = jax.nn.sigmoid(student_pre)
    back_pre = (back * logistic * (1.0 + student_pre * (1.0 - logistic))).astype(jnp.bfloat16)
    grad_in = lax.dot_general(flat, back_pre, over_tokens, preferred_element_type=jnp.float32)
    return (teacher.reshape(CLIPS, FRAMES, ROWS, WIDTH, C), grad_in, grad_out)
```

```python
import jax
import jax.numpy as jnp
from jax import lax
from jax.sharding import PartitionSpec as P


def from_behind(value, axis, by):
    count = lax.axis_size(axis)
    pairs = [(i, i + by) for i in range(count) if 0 <= i + by < count]
    return lax.ppermute(value, axis, pairs)


def extended_2(block, sides, width):
    for axis, dim in sides:
        count = lax.axis_size(axis)
        forward = [(i, i + 1) for i in range(count - 1)]
        backward = [(target, source) for source, target in forward]
        low = lax.ppermute(
            lax.slice_in_dim(block, block.shape[dim] - width, None, axis=dim), axis, forward
        )
        high = lax.ppermute(lax.slice_in_dim(block, 0, width, axis=dim), axis, backward)
        block = jnp.concatenate([low, block, high], axis=dim)
    return block


def xor_permute(value, axis, mask):
    count = lax.axis_size(axis)
    return lax.ppermute(value, axis, [(i, i ^ mask) for i in range(count)])


def gather_blocks(block):
    count = lax.axis_size("space")
    blocks = [block]
    mask = count // 2
    while mask:
        blocks = blocks + [xor_permute(b, "space", mask) for b in blocks]
        mask //= 2
    return blocks


def take_rows(value, index, rows):
    return lax.dynamic_slice_in_dim(value, index * rows, rows, axis=0)


def plane_permute(value, mask, dp_count):
    space_count = lax.axis_size("space")
    total = dp_count * space_count // 2
    pairs = []
    for member in range(total):
        other = member ^ mask
        for core in range(2):
            source = (member // (space_count // 2)) * space_count + (member % (space_count // 2)) * 2 + core
            target = (other // (space_count // 2)) * space_count + (other % (space_count // 2)) * 2 + core
            pairs.append((source, target))
    return lax.ppermute(value, ("dp", "space"), pairs)


def sum_everywhere(first, second):
    dp_count, tm_count, space_count = (lax.axis_size(a) for a in ("dp", "tm", "space"))
    space = lax.axis_index("space")
    odd = space % 2 == 1
    narrow = jnp.bfloat16
    mine = jnp.where(odd, second, first)
    yours = jnp.where(odd, first, second).astype(narrow)
    mine = mine + xor_permute(yours, "space", 1).astype(jnp.float32)
    members = dp_count * space_count // 2
    member = lax.axis_index("dp") * (space_count // 2) + space // 2
    rows = mine.shape[0] // members
    sent = mine.astype(narrow)
    arrived = [
        plane_permute(take_rows(sent, member ^ mask, rows), mask, dp_count)
        for mask in range(1, members)
    ]
    chunk = take_rows(mine, member, rows)
    for piece in arrived:
        chunk = chunk + piece.astype(jnp.float32)
    chunk = chunk.astype(narrow)
    pieces = [chunk] + [xor_permute(chunk, "tm", mask) for mask in range(1, tm_count)]
    pieces = [piece.astype(jnp.float32) for piece in pieces]
    while len(pieces) > 1:
        pieces = [pieces[i] + pieces[i + 1] for i in range(0, len(pieces), 2)]
    chunk = pieces[0].astype(narrow)
    whole = jnp.zeros(mine.shape, narrow)
    whole = lax.dynamic_update_slice_in_dim(whole, chunk, member * rows, axis=0)
    for mask in range(1, members):
        whole = lax.dynamic_update_slice_in_dim(
            whole, plane_permute(chunk, mask, dp_count), (member ^ mask) * rows, axis=0
        )
    other = xor_permute(whole, "space", 1)
    return (
        jnp.where(odd, other, whole).astype(jnp.float32),
        jnp.where(odd, whole, other).astype(jnp.float32),
    )


def root_norm(values, gain):
    return values * lax.rsqrt(jnp.mean(values * values, axis=-1, keepdims=True) + 1e-06) * gain


def attend(queries, all_keys, all_values, scale):
    scores = (
        jnp.einsum("fqc,fkc->fqk", queries, all_keys, preferred_element_type=jnp.float32) * scale
    )
    maxima = jnp.max(scores, axis=-1, keepdims=True)
    expos = jnp.exp(scores - maxima)
    totals = jnp.sum(expos, axis=-1, keepdims=True)
    weights = expos.astype(jnp.bfloat16)
    summed = jnp.einsum("fqk,fkc->fqc", weights, all_values, preferred_element_type=jnp.float32)
    return (summed / totals).astype(jnp.bfloat16)


def causal_conv(activation, weight):
    frame_count, row_count, column_count, channels = activation.shape
    earlier = from_behind(activation[frame_count - 2 :], "tm", 1)
    extended = jnp.concatenate([earlier, activation], axis=0)
    extended = extended_2(extended, (("space", 1),), 1)
    extended = jnp.pad(extended, ((0, 0), (0, 0), (1, 1), (0, 0)))
    total = jnp.zeros((frame_count * row_count * column_count, channels), jnp.float32)
    for tap_time in range(3):
        for tap_row in range(3):
            for tap_col in range(3):
                window = extended[
                    tap_time : tap_time + frame_count,
                    tap_row : tap_row + row_count,
                    tap_col : tap_col + column_count,
                ]
                total = total + jnp.dot(
                    window.reshape(-1, channels),
                    weight[tap_time, tap_row, tap_col],
                    preferred_element_type=jnp.float32,
                )
    return total


def shards(
    latent,
    attn_gain,
    w_query,
    w_key,
    w_value,
    w_out,
    conv_gain_first,
    conv_first,
    conv_gain_second,
    conv_second,
    student_in,
    student_out,
):
    frames = latent[0]
    frame_count, row_count, column_count, channels = frames.shape
    per_frame = row_count * column_count
    tokens_local = frames.reshape(-1, channels)
    inputs_wide = tokens_local.astype(jnp.float32)
    normed = root_norm(inputs_wide, attn_gain).astype(jnp.bfloat16)
    queries = (
        jnp.dot(normed, w_query, preferred_element_type=jnp.float32)
        .astype(jnp.bfloat16)
        .reshape(frame_count, per_frame, channels)
    )
    scale = channels ** (-0.5)
    piece = jnp.concatenate(
        gather_blocks(normed.reshape(frame_count, per_frame, channels)), axis=1
    )
    rows_flat = piece.reshape(-1, channels)
    piece_keys = jnp.dot(rows_flat, w_key, preferred_element_type=jnp.float32).astype(jnp.bfloat16)
    piece_values = jnp.dot(rows_flat, w_value, preferred_element_type=jnp.float32).astype(
        jnp.bfloat16
    )
    stacked = jnp.stack([piece_keys.reshape(piece.shape), piece_values.reshape(piece.shape)])
    mixed = attend(queries, stacked[0], stacked[1], scale)
    attention_out = jnp.dot(mixed.reshape(-1, channels), w_out, preferred_element_type=jnp.float32)
    mid = (inputs_wide + attention_out).astype(jnp.bfloat16)
    mid_wide = mid.astype(jnp.float32)
    first_act = jax.nn.silu(root_norm(mid_wide, conv_gain_first)).astype(jnp.bfloat16)
    first_conv = causal_conv(
        first_act.reshape(frame_count, row_count, column_count, channels), conv_first
    )
    second_act = jax.nn.silu(root_norm(first_conv, conv_gain_second)).astype(jnp.bfloat16)
    second_conv = causal_conv(
        second_act.reshape(frame_count, row_count, column_count, channels), conv_second
    )
    teacher = (mid_wide + second_conv).astype(jnp.bfloat16)
    student_pre = jnp.dot(tokens_local, student_in, preferred_element_type=jnp.float32)
    student_hidden = jax.nn.silu(student_pre).astype(jnp.bfloat16)
    predicted = inputs_wide + jnp.dot(
        student_hidden, student_out, preferred_element_type=jnp.float32
    )
    error = predicted - teacher.astype(jnp.float32)
    token_total = (
        frame_count * per_frame * lax.axis_size("dp") * lax.axis_size("tm") * lax.axis_size("space")
    )
    signal = (error * lax.rsqrt(error * error + 0.0625) * token_total ** (-0.5)).astype(
        jnp.bfloat16
    )
    over_tokens = (((0,), (0,)), ((), ()))
    local_out = lax.dot_general(
        student_hidden, signal, over_tokens, preferred_element_type=jnp.float32
    )
    back = lax.dot_general(
        signal, student_out, (((1,), (1,)), ((), ())), preferred_element_type=jnp.float32
    )
    logistic = jax.nn.sigmoid(student_pre)
    back_pre = (back * logistic * (1.0 + student_pre * (1.0 - logistic))).astype(jnp.bfloat16)
    local_in = lax.dot_general(
        tokens_local, back_pre, over_tokens, preferred_element_type=jnp.float32
    )
    grad_in, grad_out = sum_everywhere(local_in, local_out)
    return (teacher.reshape(latent.shape), grad_in, grad_out)


def solution(mesh):
    return jax.shard_map(
        shards,
        mesh=mesh,
        in_specs=(
            P("dp", "tm", "space", None, None),
            P(),
            P(),
            P(),
            P(),
            P(),
            P(),
            P(),
            P(),
            P(),
            P(),
            P(),
        ),
        out_specs=(P("dp", "tm", "space", None, None), P(), P()),
        check_vma=False,
    )
```

```python
import functools

import jax
import jax.numpy as jnp
from jax import lax
from jax.experimental import pallas as pl
from jax.experimental.pallas import tpu as pltpu
from jax.sharding import PartitionSpec as P

F32 = jnp.float32
BF16 = jnp.bfloat16
VMEM = pl.BlockSpec(memory_space=pltpu.VMEM)
ANY = pl.BlockSpec(memory_space=pl.ANY)
LIMIT = 24 << 20


def xor_permute(value, axis, mask):
    count = lax.axis_size(axis)
    return lax.ppermute(value, axis, [(i, i ^ mask) for i in range(count)])


def gather_blocks(block):
    count = lax.axis_size("space")
    blocks = [block]
    mask = count // 2
    while mask:
        blocks = blocks + [xor_permute(b, "space", mask) for b in blocks]
        mask //= 2
    return blocks


def across_permute(value):
    count = lax.axis_size("space")
    pairs = []
    for low in range(1, count - 1, 2):
        pairs += [(low, low + 1), (low + 1, low)]
    return lax.ppermute(value, "space", pairs)


def next_frames(value):
    count = lax.axis_size("tm")
    return lax.ppermute(value, "tm", [(i, i + 1) for i in range(count - 1)])


def take_rows(value, index, rows):
    return lax.dynamic_slice_in_dim(value, index * rows, rows, axis=0)


def plane_permute(value, mask, dp_count):
    chips = lax.axis_size("space") // 2
    pairs = []
    for member in range(dp_count * chips):
        other = member ^ mask
        for core in range(2):
            source = (member // chips * chips + member % chips) * 2 + core
            target = (other // chips * chips + other % chips) * 2 + core
            pairs.append((source, target))
    return lax.ppermute(value, ("dp", "space"), pairs)


def sum_everywhere(mine, yours, odd):
    dp_count, tm_count, space_count = (lax.axis_size(a) for a in ("dp", "tm", "space"))
    mine = mine + xor_permute(yours, "space", 1).astype(F32)
    members = dp_count * space_count // 2
    member = lax.axis_index("dp") * (space_count // 2) + lax.axis_index("space") // 2
    rows = mine.shape[0] // members
    sent = mine.astype(BF16)
    arrived = [
        plane_permute(take_rows(sent, member ^ mask, rows), mask, dp_count)
        for mask in range(1, members)
    ]
    chunk = take_rows(mine, member, rows)
    for piece in arrived:
        chunk = chunk + piece.astype(F32)
    chunk = chunk.astype(BF16)
    pieces = [chunk] + [xor_permute(chunk, "tm", mask) for mask in range(1, tm_count)]
    pieces = [piece.astype(F32) for piece in pieces]
    while len(pieces) > 1:
        pieces = [pieces[i] + pieces[i + 1] for i in range(0, len(pieces), 2)]
    chunk = pieces[0].astype(BF16)
    whole = jnp.zeros(mine.shape, BF16)
    whole = lax.dynamic_update_slice_in_dim(whole, chunk, member * rows, axis=0)
    for mask in range(1, members):
        whole = lax.dynamic_update_slice_in_dim(
            whole, plane_permute(chunk, mask, dp_count), (member ^ mask) * rows, axis=0
        )
    other = xor_permute(whole, "space", 1)
    return (
        jnp.where(odd, other, whole).astype(F32),
        jnp.where(odd, whole, other).astype(F32),
    )


def root_norm(values, gain):
    return values * lax.rsqrt(jnp.mean(values * values, axis=-1, keepdims=True) + 1e-06) * gain


def silu(values):
    return values * jax.nn.sigmoid(values)


def dot(left, right):
    return jnp.dot(left, right, preferred_element_type=F32)


def call(body, outs, specs, out_specs, scratch, flops, moved, *args):
    return pl.pallas_call(
        body,
        out_shape=outs,
        in_specs=specs,
        out_specs=out_specs,
        scratch_shapes=scratch,
        compiler_params=pltpu.CompilerParams(vmem_limit_bytes=LIMIT),
        cost_estimate=pl.CostEstimate(
            flops=int(flops), bytes_accessed=int(moved), transcendentals=0
        ),
    )(*args)


def shape(rows, columns, dtype):
    return jax.ShapeDtypeStruct((rows, columns), dtype)


def put_edges(values, columns, odd, on_ref, off_ref, at):
    first, last = values[:columns], values[values.shape[0] - columns :]
    where = pl.ds(at * columns, columns)
    on_ref[where] = jnp.where(odd, first, last)
    off_ref[where] = jnp.where(odd, last, first)


def norm_body(frame_count, latent, gain, *normed):
    for frame in range(frame_count):
        wide = latent[frame].astype(F32)
        normed[frame][...] = root_norm(wide, gain[...]).astype(BF16)


def student_body(latent, s_in, s_out, pre, hidden_t, latent_t, predicted):
    tokens = latent[...]
    before = dot(tokens, s_in[...])
    hidden = silu(before).astype(BF16)
    pre[...] = before
    predicted[...] = tokens.astype(F32) + dot(hidden, s_out[...])
    hidden_t[...] = hidden.T
    latent_t[...] = tokens.T


def attend_body(blocks, columns, weighted, odd_ref, *refs):
    parts, refs = refs[:blocks], refs[blocks:]
    latent, w_query, w_key, w_value, w_out, gain, refs = *refs[:6], refs[6:]
    channels = w_query.shape[0]
    if weighted:
        taps, (act, mid, on, off, packed, sem) = refs[0], refs[1:]
        copies = [
            pltpu.make_async_copy(
                taps.at[t, r, c],
                packed.at[t, pl.ds(r * channels, channels), pl.ds(c * channels, channels)],
                sem.at[0],
            )
            for t in range(3)
            for r in range(3)
            for c in range(3)
        ]
        for copy in copies:
            copy.start()
    else:
        act, mid, on, off = refs
    odd = odd_ref[0] == 1
    rows = jnp.concatenate([part[...] for part in parts], axis=0)
    queries = dot(parts[0][...], w_query[...]).astype(BF16)
    keys = dot(rows, w_key[...]).astype(BF16)
    values = dot(rows, w_value[...]).astype(BF16)
    scores = lax.dot_general(
        queries, keys, (((1,), (1,)), ((), ())), preferred_element_type=F32
    ) * channels ** (-0.5)
    expos = jnp.exp(scores - jnp.max(scores, axis=-1, keepdims=True))
    totals = jnp.sum(expos, axis=-1, keepdims=True)
    mixed = (dot(expos.astype(BF16), values) / totals).astype(BF16)
    middle = (latent[...].astype(F32) + dot(mixed, w_out[...])).astype(BF16)
    mid[...] = middle
    active = silu(root_norm(middle.astype(F32), gain[...])).astype(BF16)
    act[...] = active
    put_edges(active, columns, odd, on, off, 0)
    if weighted:
        for copy in copies:
            copy.wait()


def edges_body(columns, odd_ref, frames, on, off):
    odd = odd_ref[0] == 1
    per_frame = frames.shape[0] // (on.shape[0] // columns)
    for at in range(on.shape[0] // columns):
        put_edges(frames[pl.ds(at * per_frame, per_frame)], columns, odd, on, off, at)


def stack_rows(columns, odd, own, on, off, stacked, at):
    per_frame, channels = own.shape
    base = at * per_frame
    split = per_frame - columns
    stacked[pl.ds(base, columns), 0:channels] = jnp.where(odd, on, off)
    stacked[pl.ds(base + columns, split), 0:channels] = own[:split]
    stacked[pl.ds(base, per_frame), channels : 2 * channels] = own
    stacked[pl.ds(base, split), 2 * channels :] = own[columns:]
    stacked[pl.ds(base + split, columns), 2 * channels :] = jnp.where(odd, off, on)


def taps_sum(sources, frame, stacked, packed, per_frame, total):
    for at, source in enumerate(sources):
        tap = source - frame
        if 0 <= tap < 3:
            term = dot(stacked[pl.ds(at * per_frame, per_frame)], packed[tap])
            total = term if total is None else total + term
    return total


def shift_columns(total, columns):
    rows, channels = total.shape[0], total.shape[1] // 3
    column = lax.broadcasted_iota(jnp.int32, (rows, channels), 0) % columns
    before = pltpu.roll(total[:, :channels], 1, 0)
    after = pltpu.roll(total[:, 2 * channels :], rows - 1, 0)
    return (
        total[:, channels : 2 * channels]
        + jnp.where(column == 0, 0.0, before)
        + jnp.where(column == columns - 1, 0.0, after)
    )


def load_sources(groups, columns, odd, refs, stacked):
    at = 0
    for group in range(len(groups)):
        own, on, off = refs[3 * group : 3 * group + 3]
        per_frame = own.shape[0] // groups[group]
        for frame in range(groups[group]):
            edge = pl.ds(frame * columns, columns)
            stack_rows(
                columns, odd, own[pl.ds(frame * per_frame, per_frame)], on[edge], off[edge],
                stacked, at,
            )
            at += 1
    return per_frame


def part_body(groups, sources, frame_count, columns, odd_ref, *refs):
    odd = odd_ref[0] == 1
    packed, partial, stacked = refs[-3:]
    per_frame = load_sources(groups, columns, odd, refs[:-3], stacked)
    for frame in range(frame_count):
        total = taps_sum(sources, frame, stacked, packed, per_frame, None)
        partial[pl.ds(frame * per_frame, per_frame)] = total


def first_body(groups, sources, frame_count, columns, odd_ref, *refs):
    odd = odd_ref[0] == 1
    count = 3 * len(groups)
    packed, partial, gain, act, tail, on, off, stacked = refs[count:]
    per_frame = load_sources(groups, columns, odd, refs[:count], stacked)
    for frame in range(frame_count - 1, -1, -1):
        here = pl.ds(frame * per_frame, per_frame)
        total = taps_sum(sources, frame, stacked, packed, per_frame, partial[here])
        total = shift_columns(total, columns)
        active = silu(root_norm(total, gain[...])).astype(BF16)
        act[here] = active
        if frame >= frame_count - 2:
            tail[pl.ds((frame - frame_count + 2) * per_frame, per_frame)] = active
        put_edges(active, columns, odd, on, off, frame)


def last_body(groups, sources, frame_count, columns, token_total, odd_ref, *refs):
    odd = odd_ref[0] == 1
    count = 3 * len(groups)
    mids = refs[count + 2 : count + 2 + frame_count]
    packed, partial = refs[count : count + 2]
    pre, hidden_t, latent_t, predicted, s_out = refs[count + 2 + frame_count :][:5]
    teacher, mine, yours, stacked, signals = refs[count + 7 + frame_count :]
    per_frame = load_sources(groups, columns, odd, refs[:count], stacked)
    for frame in range(frame_count - 1, -1, -1):
        here = pl.ds(frame * per_frame, per_frame)
        total = taps_sum(sources, frame, stacked, packed, per_frame, partial[here])
        total = shift_columns(total, columns)
        taught = (mids[frame][...].astype(F32) + total).astype(BF16)
        teacher[here] = taught
        error = predicted[here] - taught.astype(F32)
        signals[here] = (
            error * lax.rsqrt(error * error + 0.0625) * token_total ** (-0.5)
        ).astype(BF16)
    signal = signals[...]
    grad_out = dot(hidden_t[...], signal)
    back = lax.dot_general(
        signal, s_out[...], (((1,), (1,)), ((), ())), preferred_element_type=F32
    )
    before = pre[...]
    logistic = jax.nn.sigmoid(before)
    back_pre = (back * logistic * (1.0 + before * (1.0 - logistic))).astype(BF16)
    grad_in = dot(latent_t[...], back_pre)
    mine[...] = jnp.where(odd, grad_out, grad_in)
    yours[...] = jnp.where(odd, grad_in, grad_out).astype(BF16)


def shards(
    latent,
    attn_gain,
    w_query,
    w_key,
    w_value,
    w_out,
    conv_gain_first,
    conv_first,
    conv_gain_second,
    conv_second,
    student_in,
    student_out,
):
    frame_count, row_count, columns, channels = latent.shape[1:]
    per_frame = row_count * columns
    tokens = frame_count * per_frame
    frames = latent.reshape(frame_count, per_frame, channels)
    attn_gain, conv_gain_first, conv_gain_second = (
        gain.reshape(1, channels) for gain in (attn_gain, conv_gain_first, conv_gain_second)
    )
    odd = (lax.axis_index("space") % 2).astype(jnp.int32)
    odd_flag = odd.reshape(1)
    smem = pl.BlockSpec(memory_space=pltpu.SMEM)
    unit = 2 * channels * channels
    frame_bf = shape(per_frame, channels, BF16)
    edge_bf = shape(columns, channels, BF16)

    normed = call(
        functools.partial(norm_body, frame_count),
        [frame_bf] * frame_count, [VMEM] * 2, [VMEM] * frame_count, [],
        0, 4 * tokens * channels, frames, attn_gain,
    )
    order = list(range(frame_count - 1, -1, -1))
    gathered = {frame: gather_blocks(normed[frame]) for frame in order}

    pre, hidden_t, latent_t, predicted = call(
        student_body,
        [shape(tokens, channels, F32), shape(channels, tokens, BF16),
         shape(channels, tokens, BF16), shape(tokens, channels, F32)],
        [VMEM] * 3, [VMEM] * 4, [],
        2 * tokens * unit, 4 * tokens * channels,
        frames.reshape(tokens, channels), student_in, student_out,
    )

    packed_shape = jax.ShapeDtypeStruct((3, 3 * channels, 3 * channels), BF16)
    weights = [conv_first, conv_second]
    packed, acts, mids, ons, offs = [], {}, {}, {}, {}
    for turn, frame in enumerate(order):
        blocks = gathered[frame]
        weighted = turn < 2
        outs = [frame_bf, frame_bf, edge_bf, edge_bf]
        args = [
            odd_flag, *blocks, frames[frame], w_query, w_key, w_value, w_out, conv_gain_first
        ]
        specs = [smem] + [VMEM] * (len(args) - 1)
        scratch = []
        if weighted:
            args.append(weights[turn])
            specs.append(ANY)
            outs.append(packed_shape)
            scratch.append(pltpu.SemaphoreType.DMA((1,)))
        result = call(
            functools.partial(attend_body, len(blocks), columns, weighted),
            outs, specs, [VMEM] * len(outs), scratch,
            (2 + 4 * len(blocks)) * per_frame * unit, 4 * per_frame * channels, *args,
        )
        acts[frame], mids[frame], ons[frame], offs[frame] = result[:4]
        if weighted:
            packed.append(result[4])

    def halo(on, off):
        return xor_permute(on, "space", 1), across_permute(off)

    def forwarded(tail, count):
        on, off = call(
            functools.partial(edges_body, columns),
            [shape(count * columns, channels, BF16)] * 2, [smem, VMEM], [VMEM] * 2, [],
            0, 2 * per_frame * channels, odd_flag, tail,
        )
        return (tail, *halo(on, off))

    def stacked(count):
        return pltpu.VMEM((count * per_frame, 3 * channels), BF16)

    partial_shape = shape(tokens, 3 * channels, F32)
    edges_shape = shape(frame_count * columns, channels, BF16)

    early = [(acts[f], *halo(ons[f], offs[f])) for f in range(1, frame_count)]
    tails = [forwarded(next_frames(acts[f]), 1) for f in (frame_count - 2, frame_count - 1)]
    late = (acts[0], *halo(ons[0], offs[0]))
    groups = [1] * (frame_count + 1)
    sources = [0, 1] + list(range(3, frame_count + 2))
    args = [odd_flag, *(ref for group in tails + early for ref in group), packed[0]]
    partial = call(
        functools.partial(part_body, groups, sources, frame_count, columns),
        partial_shape, [smem] + [VMEM] * (len(args) - 1), VMEM, [stacked(frame_count + 1)],
        18 * tokens * unit, 8 * tokens * channels, *args,
    )
    args = [odd_flag, *late, packed[0], partial, conv_gain_second]
    act, tail, on, off = call(
        functools.partial(first_body, [1], [2], frame_count, columns),
        [shape(tokens, channels, BF16), shape(2 * per_frame, channels, BF16),
         edges_shape, edges_shape],
        [smem] + [VMEM] * (len(args) - 1), [VMEM] * 4, [stacked(1)],
        9 * tokens * unit, 8 * tokens * channels, *args,
    )

    tail = next_frames(tail)
    own = (act, *halo(on, off))
    args = [odd_flag, *own, packed[1]]
    partial = call(
        functools.partial(
            part_body, [frame_count], list(range(2, frame_count + 2)), frame_count, columns
        ),
        partial_shape, [smem] + [VMEM] * (len(args) - 1), VMEM, [stacked(frame_count)],
        18 * tokens * unit, 8 * tokens * channels, *args,
    )
    token_total = tokens * lax.axis_size("dp") * lax.axis_size("tm") * lax.axis_size("space")
    args = [
        odd_flag, *forwarded(tail, 2), packed[1], partial, *(mids[f] for f in range(frame_count)),
        pre, hidden_t, latent_t, predicted, student_out,
    ]
    square = shape(channels, channels, F32)
    teacher, mine, yours = call(
        functools.partial(last_body, [2], [0, 1], frame_count, columns, token_total),
        [shape(tokens, channels, BF16), square, shape(channels, channels, BF16)],
        [smem] + [VMEM] * (len(args) - 1), [VMEM] * 3,
        [stacked(2), pltpu.VMEM((tokens, channels), BF16)],
        12 * tokens * unit, 8 * tokens * channels, *args,
    )
    grad_in, grad_out = sum_everywhere(mine, yours, odd == 1)
    return (teacher.reshape(latent.shape), grad_in, grad_out)


def solution(mesh):
    return jax.shard_map(
        shards,
        mesh=mesh,
        in_specs=(
            P("dp", "tm", "space", None, None),
            P(),
            P(),
            P(),
            P(),
            P(),
            P(),
            P(),
            P(),
            P(),
            P(),
            P(),
        ),
        out_specs=(P("dp", "tm", "space", None, None), P(), P()),
        check_vma=False,
    )
```

```python
import functools

import jax
import jax.numpy as jnp
from jax import lax
from jax.experimental import pallas as pl
from jax.experimental.pallas import tpu as pltpu
from jax.sharding import PartitionSpec as P


F32 = jnp.float32
BF16 = jnp.bfloat16
VMEM = pl.BlockSpec(memory_space=pltpu.VMEM)
HBM = pl.BlockSpec(memory_space=pltpu.HBM)
LIMIT = 20 << 20


def xor_permute(value, axis, mask):
    count = lax.axis_size(axis)
    return lax.ppermute(value, axis, [(i, i ^ mask) for i in range(count)])


def gather_blocks(block):
    mask = lax.axis_size("space") // 2
    blocks = [block, xor_permute(block, "space", mask)]
    while mask > 1:
        mask //= 2
        blocks = blocks + [xor_permute(b, "space", mask) for b in blocks]
    return blocks


def across_pairs():
    pairs = []
    for low in range(1, lax.axis_size("space") - 1, 2):
        pairs += [(low, low + 1), (low + 1, low)]
    return pairs


def across_permute(value):
    return lax.ppermute(value, "space", across_pairs())


def across_next_frames(value):
    count = lax.axis_size("space")
    pairs = [
        (block * count + source, (block + 1) * count + target)
        for block in range(lax.axis_size("tm") - 1)
        for source, target in across_pairs()
    ]
    return lax.ppermute(value, ("tm", "space"), pairs)


def next_frames(value):
    count = lax.axis_size("tm")
    return lax.ppermute(value, "tm", [(i, i + 1) for i in range(count - 1)])


def take_rows(value, index, rows):
    return lax.dynamic_slice_in_dim(value, index * rows, rows, axis=0)


def plane_permute(value, mask, dp_count):
    chips = lax.axis_size("space") // 2
    pairs = []
    for member in range(dp_count * chips):
        other = member ^ mask
        for core in range(2):
            source = (member // chips * chips + member % chips) * 2 + core
            target = (other // chips * chips + other % chips) * 2 + core
            pairs.append((source, target))
    return lax.ppermute(value, ("dp", "space"), pairs)


def sum_everywhere(mine, yours):
    odd = is_odd()
    dp_count, tm_count, space_count = (lax.axis_size(a) for a in ("dp", "tm", "space"))
    mine = mine + xor_permute(yours, "space", 1).astype(F32)
    members = dp_count * space_count // 2
    member = lax.axis_index("dp") * (space_count // 2) + lax.axis_index("space") // 2
    rows = mine.shape[0] // members
    sent = mine.astype(BF16)
    arrived = [
        plane_permute(take_rows(sent, member ^ mask, rows), mask, dp_count)
        for mask in range(1, members)
    ]
    chunk = take_rows(mine, member, rows)
    for piece in arrived:
        chunk = chunk + piece.astype(F32)
    chunk = chunk.astype(BF16)
    pieces = [chunk] + [xor_permute(chunk, "tm", mask) for mask in range(1, tm_count)]
    pieces = [piece.astype(F32) for piece in pieces]
    while len(pieces) > 1:
        pieces = [pieces[i] + pieces[i + 1] for i in range(0, len(pieces), 2)]
    chunk = pieces[0].astype(BF16)
    whole = jnp.zeros(mine.shape, BF16)
    whole = lax.dynamic_update_slice_in_dim(whole, chunk, member * rows, axis=0)
    for mask in range(1, members):
        whole = lax.dynamic_update_slice_in_dim(
            whole, plane_permute(chunk, mask, dp_count), (member ^ mask) * rows, axis=0
        )
    other = xor_permute(whole, "space", 1)
    return (
        jnp.where(odd, other, whole).astype(F32),
        jnp.where(odd, whole, other).astype(F32),
    )


def root_norm(values, gain):
    return values * lax.rsqrt(jnp.mean(values * values, axis=-1, keepdims=True) + 1e-06) * gain


def silu(values):
    return values * jax.nn.sigmoid(values)


def dot(left, right):
    return jnp.dot(left, right, preferred_element_type=F32)


def call(body, outs, specs, out_specs, scratch, flops, moved, *args):
    return pl.pallas_call(
        body,
        out_shape=outs,
        in_specs=specs,
        out_specs=out_specs,
        scratch_shapes=scratch,
        compiler_params=pltpu.CompilerParams(vmem_limit_bytes=LIMIT),
        cost_estimate=pl.CostEstimate(
            flops=int(flops), bytes_accessed=int(moved), transcendentals=0
        ),
    )(*(
        pltpu.with_memory_space_constraint(arg, pltpu.HBM) if spec is HBM else arg
        for arg, spec in zip(args, specs, strict=True)
    ))


def shape(rows, columns, dtype):
    return jax.ShapeDtypeStruct((rows, columns), dtype)


def is_odd():
    return lax.rem(lax.axis_index("space"), 2) == 1


def edge_rows(values, columns, odd):
    first, last = values[:columns], values[values.shape[0] - columns :]
    return jnp.where(odd, first, last), jnp.where(odd, last, first)


def norm_body(late, latent_hbm, gain_hbm, latent, normed_late, normed_early, gain, sems):
    frame_count, per_frame = latent_hbm.shape[:2]
    pltpu.make_async_copy(gain_hbm, gain, sems.at[frame_count]).start()
    copies = {}
    for frame in range(frame_count - 1, -1, -1):
        here = pl.ds(frame * per_frame, per_frame)
        copies[frame] = pltpu.make_async_copy(latent_hbm.at[frame], latent.at[here], sems.at[frame])
        copies[frame].start()
    pltpu.make_async_copy(gain_hbm, gain, sems.at[frame_count]).wait()
    for frame in range(frame_count - 1, -1, -1):
        copies[frame].wait()
        wide = latent[pl.ds(frame * per_frame, per_frame)].astype(F32)
        normed = root_norm(wide, gain[...].reshape(1, -1)).astype(BF16)
        at = frame - (frame_count - late)
        target = normed_late if at >= 0 else normed_early
        target[pl.ds((at if at >= 0 else frame) * per_frame, per_frame)] = normed


def prepare_body(
    latent, query_hbm, key_hbm, value_hbm, out_hbm, in_hbm, back_hbm, first_hbm, second_hbm,
    w_query, w_both, w_out, s_out, first, second, pre, hidden_t, latent_t, predicted,
    s_in, sems,
):
    channels = latent.shape[1]
    student = [
        pltpu.make_async_copy(in_hbm, s_in, sems.at[0]),
        pltpu.make_async_copy(back_hbm, s_out, sems.at[1]),
    ]
    rest = [
        pltpu.make_async_copy(query_hbm, w_query, sems.at[2]),
        pltpu.make_async_copy(key_hbm, w_both.at[:, pl.ds(0, channels)], sems.at[3]),
        pltpu.make_async_copy(value_hbm, w_both.at[:, pl.ds(channels, channels)], sems.at[4]),
        pltpu.make_async_copy(out_hbm, w_out, sems.at[5]),
    ]
    for at, (taps, packed) in enumerate(((first_hbm, first), (second_hbm, second))):
        for t in range(3):
            for r in range(3):
                for c in range(3):
                    block = packed.at[t, pl.ds(r * channels, channels), pl.ds(c * channels, channels)]
                    rest.append(
                        pltpu.make_async_copy(taps.at[t, r, c], block, sems.at[6 + 3 * at + t])
                    )
    for copy in student + rest:
        copy.start()
    tokens = latent[...]
    latent_t[...] = tokens.T
    student[0].wait()
    before = dot(tokens, s_in[...])
    hidden = silu(before).astype(BF16)
    pre[...] = before
    hidden_t[...] = hidden.T
    student[1].wait()
    predicted[...] = tokens.astype(F32) + dot(hidden, s_out[...])
    for copy in rest:
        copy.wait()


def attend_body(blocks, start, count, later, columns, *refs):
    parts = refs[:blocks]
    latent, w_query, w_both, w_out, gain = refs[blocks : blocks + 5]
    act, mid, on, off = refs[-4:]
    channels = w_query.shape[0]
    odd = is_odd()
    per_frame = parts[0].shape[0] // count
    if later:
        for ends, others in zip((on, off), refs[blocks + 5 : -4], strict=True):
            ends[pl.ds(count * columns, others.shape[0])] = others[...]
    for frame in range(count - 1, -1, -1):
        here = pl.ds(frame * per_frame, per_frame)
        rows = jnp.concatenate([part[here] for part in parts], axis=0)
        queries = dot(parts[0][here], w_query[...]).astype(BF16)
        both = dot(rows, w_both[...]).astype(BF16)
        keys, values = both[:, :channels], both[:, channels:]
        scores = lax.dot_general(
            queries, keys, (((1,), (1,)), ((), ())), preferred_element_type=F32
        ) * channels ** (-0.5)
        expos = jnp.exp(scores - jnp.max(scores, axis=-1, keepdims=True))
        totals = jnp.sum(expos, axis=-1, keepdims=True)
        mixed = (dot(expos.astype(BF16), values) / totals).astype(BF16)
        own = latent[pl.ds((start + frame) * per_frame, per_frame)]
        middle = (own.astype(F32) + dot(mixed, w_out[...])).astype(BF16)
        mid[here] = middle
        active = silu(root_norm(middle.astype(F32), gain[...].reshape(1, -1))).astype(BF16)
        act[here] = active
        edge = pl.ds(frame * columns, columns)
        on[edge], off[edge] = edge_rows(active, columns, odd)


def stack_rows(columns, odd, own, on, off, stacked, at):
    per_frame, channels = own.shape
    base = at * per_frame
    split = per_frame - columns
    stacked[pl.ds(base, columns), 0:channels] = jnp.where(odd, on, off)
    stacked[pl.ds(base + columns, split), 0:channels] = own[:split]
    stacked[pl.ds(base, per_frame), channels : 2 * channels] = own
    stacked[pl.ds(base, split), 2 * channels :] = own[columns:]
    stacked[pl.ds(base + split, columns), 2 * channels :] = jnp.where(odd, off, on)


def taps_sum(sources, frame, stacked, packed, per_frame, total):
    for at, source in enumerate(sources):
        tap = source - frame
        if 0 <= tap < 3:
            term = dot(stacked[pl.ds(at * per_frame, per_frame)], packed[tap])
            total = term if total is None else total + term
    return total


def shift_columns(total, columns):
    rows, channels = total.shape[0], total.shape[1] // 3
    column = lax.broadcasted_iota(jnp.int32, (rows, channels), 0) % columns
    before = pltpu.roll(total[:, :channels], 1, 0)
    after = pltpu.roll(total[:, 2 * channels :], rows - 1, 0)
    return (
        total[:, channels : 2 * channels]
        + jnp.where(column == 0, 0.0, before)
        + jnp.where(column == columns - 1, 0.0, after)
    )


def own_body(groups, columns, *refs):
    odd = is_odd()
    off, on, packed, partial, stacked = refs[-5:]
    frame_count = sum(groups)
    per_frame = partial.shape[0] // frame_count
    at = 0
    for own, frames in zip(refs[:-5], groups, strict=True):
        for frame in range(frames):
            edge = pl.ds(at * columns, columns)
            stack_rows(
                columns, odd, own[pl.ds(frame * per_frame, per_frame)], on[edge], off[edge],
                stacked, at,
            )
            at += 1
    sources = range(2, frame_count + 2)
    for frame in range(frame_count):
        total = taps_sum(sources, frame, stacked, packed, per_frame, None)
        partial[pl.ds(frame * per_frame, per_frame)] = total


def stack_earlier(columns, odd, tail, partner, off, stacked):
    per_frame = stacked.shape[0] // 2
    for frame in range(2):
        here = pl.ds(frame * per_frame, per_frame)
        on, _ = edge_rows(partner[here], columns, jnp.logical_not(odd))
        edge = pl.ds(frame * columns, columns)
        stack_rows(columns, odd, tail[here], on, off[edge], stacked, frame)


def first_body(
    columns, tail, partner, tail_off, packed, partial, gain, act, late, on, off,
    off_late, stacked,
):
    odd = is_odd()
    stack_earlier(columns, odd, tail, partner, tail_off, stacked)
    per_frame = stacked.shape[0] // 2
    frame_count = partial.shape[0] // per_frame
    for frame in range(frame_count - 1, -1, -1):
        here = pl.ds(frame * per_frame, per_frame)
        total = taps_sum((0, 1), frame, stacked, packed, per_frame, partial[here])
        total = shift_columns(total, columns)
        active = silu(root_norm(total, gain[...].reshape(1, -1))).astype(BF16)
        act[here] = active
        edge = pl.ds(frame * columns, columns)
        near, far = edge_rows(active, columns, odd)
        on[edge], off[edge] = near, far
        at = frame - (frame_count - 2)
        if at >= 0:
            late[pl.ds(at * per_frame, per_frame)] = active
            off_late[pl.ds(at * columns, columns)] = far


def last_body(
    columns, token_total, tail, partner, tail_off, packed, partial, mid_early, mid_late,
    pre, hidden_t, latent_t, predicted, s_out, teacher, mine, yours, stacked, signals,
):
    odd = is_odd()
    stack_earlier(columns, odd, tail, partner, tail_off, stacked)
    per_frame = stacked.shape[0] // 2
    frame_count = partial.shape[0] // per_frame
    for frame in range(frame_count - 1, -1, -1):
        here = pl.ds(frame * per_frame, per_frame)
        total = taps_sum((0, 1), frame, stacked, packed, per_frame, partial[here])
        total = shift_columns(total, columns)
        at = frame - (frame_count - 2)
        mid = mid_late[pl.ds(at * per_frame, per_frame)] if at >= 0 else mid_early[here]
        taught = (mid.astype(F32) + total).astype(BF16)
        teacher[here] = taught
        error = predicted[here] - taught.astype(F32)
        signals[here] = (
            error * lax.rsqrt(error * error + 0.0625) * token_total ** (-0.5)
        ).astype(BF16)
    signal = signals[...]
    grad_out = dot(hidden_t[...], signal)
    back = lax.dot_general(
        signal, s_out[...], (((1,), (1,)), ((), ())), preferred_element_type=F32
    )
    before = pre[...]
    logistic = jax.nn.sigmoid(before)
    back_pre = (back * logistic * (1.0 + before * (1.0 - logistic))).astype(BF16)
    grad_in = dot(latent_t[...], back_pre)
    mine[...] = jnp.where(odd, grad_out, grad_in)
    yours[...] = jnp.where(odd, grad_in, grad_out).astype(BF16)


def shards(
    latent,
    attn_gain,
    w_query,
    w_key,
    w_value,
    w_out,
    conv_gain_first,
    conv_first,
    conv_gain_second,
    conv_second,
    student_in,
    student_out,
):
    frame_count, row_count, columns, channels = latent.shape[1:]
    per_frame = row_count * columns
    tokens = frame_count * per_frame
    early = frame_count - 2
    frames = latent.reshape(frame_count, per_frame, channels)
    unit = 2 * channels * channels
    square = shape(channels, channels, BF16)

    def rows_of(count):
        return shape(count * per_frame, channels, BF16)

    def edges_of(count):
        return shape(count * columns, channels, BF16)

    latent_rows, normed_late, normed_early = call(
        functools.partial(norm_body, 2),
        [rows_of(frame_count), rows_of(2), rows_of(early)], [HBM] * 2, [VMEM] * 3,
        [pltpu.VMEM((channels,), F32), pltpu.SemaphoreType.DMA((frame_count + 1,))],
        0, 4 * tokens * channels, frames, attn_gain,
    )
    blocks_late = gather_blocks(normed_late)
    blocks_early = gather_blocks(normed_early)

    packed_shape = jax.ShapeDtypeStruct((3, 3 * channels, 3 * channels), BF16)
    wide = shape(tokens, channels, F32)
    turned = shape(channels, tokens, BF16)
    weights = (w_query, w_key, w_value, w_out, student_in, student_out, conv_first, conv_second)
    (
        w_query, w_both, w_out, student_out, packed_first, packed_second,
        pre, hidden_t, latent_t, predicted,
    ) = call(
        prepare_body,
        [square, shape(channels, 2 * channels, BF16), square, square, packed_shape, packed_shape,
         wide, turned, turned, wide],
        [VMEM] + [HBM] * len(weights), [VMEM] * 10,
        [pltpu.VMEM((channels, channels), BF16), pltpu.SemaphoreType.DMA((12,))],
        2 * tokens * unit, 60 * channels * channels * 2, latent_rows, *weights,
    )

    def attend(blocks, start, count, *others):
        args = [*blocks, latent_rows, w_query, w_both, w_out, conv_gain_first, *others]
        ends = edges_of(count + 2 if others else count)
        return call(
            functools.partial(attend_body, len(blocks), start, count, bool(others), columns),
            [rows_of(count), rows_of(count), ends, ends],
            [VMEM] * len(args), [VMEM] * 4, [],
            (2 + 4 * len(blocks)) * count * per_frame * unit, 4 * count * per_frame * channels,
            *args,
        )

    def stacked(count):
        return pltpu.VMEM((count * per_frame, 3 * channels), BF16)

    def from_earlier(late, off):
        tail = next_frames(late)
        corner = across_next_frames(off)
        partner = xor_permute(tail, "space", 1)
        return tail, corner, partner

    def own_part(groups, on, off, packed):
        halo = [across_permute(off), xor_permute(on, "space", 1)]
        args = [*(own for _, own in groups), *halo, packed]
        return call(
            functools.partial(own_body, [group[0] for group in groups], columns),
            shape(tokens, 3 * channels, F32), [VMEM] * len(args), VMEM,
            [stacked(frame_count)], 18 * tokens * unit, 8 * tokens * channels, *args,
        )

    act_late, mid_late, on_late, off_late = attend(blocks_late, early, 2)
    tail, tail_off, partner = from_earlier(act_late, off_late)
    act_early, mid_early, on, off = attend(blocks_early, 0, early, on_late, off_late)
    partial = own_part([(early, act_early), (2, act_late)], on, off, packed_first)
    args = [tail, partner, tail_off, packed_first, partial, conv_gain_second]
    act, late, on, off, off_late = call(
        functools.partial(first_body, columns),
        [rows_of(frame_count), rows_of(2), edges_of(frame_count), edges_of(frame_count), edges_of(2)],
        [VMEM] * len(args), [VMEM] * 5, [stacked(2)],
        9 * tokens * unit, 8 * tokens * channels, *args,
    )
    tail, tail_off, partner = from_earlier(late, off_late)
    partial = own_part([(frame_count, act)], on, off, packed_second)
    token_total = tokens * lax.axis_size("dp") * lax.axis_size("tm") * lax.axis_size("space")
    args = [
        tail, partner, tail_off, packed_second, partial, mid_early, mid_late,
        pre, hidden_t, latent_t, predicted, student_out,
    ]
    teacher, mine, yours = call(
        functools.partial(last_body, columns, token_total),
        [rows_of(frame_count), shape(channels, channels, F32), square],
        [VMEM] * len(args), [VMEM] * 3,
        [stacked(2), pltpu.VMEM((tokens, channels), BF16)],
        12 * tokens * unit, 8 * tokens * channels, *args,
    )
    grad_in, grad_out = sum_everywhere(mine, yours)
    return (teacher.reshape(latent.shape), grad_in, grad_out)


def solution(mesh):
    return jax.shard_map(
        shards,
        mesh=mesh,
        in_specs=(
            P("dp", "tm", "space", None, None),
            P(),
            P(),
            P(),
            P(),
            P(),
            P(),
            P(),
            P(),
            P(),
            P(),
            P(),
        ),
        out_specs=(P("dp", "tm", "space", None, None), P(), P()),
        check_vma=False,
    )
```

```python
import functools

import jax
import jax.numpy as jnp
from jax import lax
from jax.experimental import pallas as pl
from jax.experimental.pallas import tpu as pltpu
from jax.sharding import PartitionSpec as P


F32 = jnp.float32
BF16 = jnp.bfloat16
VMEM = pl.BlockSpec(memory_space=pltpu.VMEM)
HBM = pl.BlockSpec(memory_space=pltpu.HBM)
LIMIT = 20 << 20


def xor_permute(value, axis, mask):
    count = lax.axis_size(axis)
    return lax.ppermute(value, axis, [(i, i ^ mask) for i in range(count)])


def gather_blocks(block):
    mask = lax.axis_size("space") // 2
    blocks = [block, xor_permute(block, "space", mask)]
    while mask > 1:
        mask //= 2
        blocks = blocks + [xor_permute(b, "space", mask) for b in blocks]
    return blocks


def across_pairs():
    pairs = []
    for low in range(1, lax.axis_size("space") - 1, 2):
        pairs += [(low, low + 1), (low + 1, low)]
    return pairs


def across_permute(value):
    clips, count = lax.axis_size("dp"), lax.axis_size("space")
    rows = dict(across_pairs())
    pairs = []
    for clip in range(clips):
        for place in range(count):
            other = (clip, rows[place]) if place in rows else (clip ^ 1, place)
            if other[0] < clips:
                pairs.append((clip * count + place, other[0] * count + other[1]))
    return lax.ppermute(value, ("dp", "space"), pairs)


def across_next_frames(value):
    count = lax.axis_size("space")
    pairs = [
        (block * count + source, (block + 1) * count + target)
        for block in range(lax.axis_size("tm") - 1)
        for source, target in across_pairs()
    ]
    return lax.ppermute(value, ("tm", "space"), pairs)


def frame_pairings(value):
    blocks, count = lax.axis_size("tm"), lax.axis_size("space")
    results = []
    for first in range(2):
        pairs = []
        for block in range(blocks):
            other = ((block - first) ^ 1) + first
            for place in range(count):
                inside = 0 <= other < blocks
                target = other * count + place if inside else block * count + (place ^ 1)
                pairs.append((block * count + place, target))
        results.append(lax.ppermute(value, ("tm", "space"), pairs))
    return results


def take_rows(value, index, rows):
    return lax.dynamic_slice_in_dim(value, index * rows, rows, axis=0)


def plane_permute(value, mask, dp_count):
    chips = lax.axis_size("space") // 2
    pairs = []
    for member in range(dp_count * chips):
        other = member ^ mask
        for core in range(2):
            source = (member // chips * chips + member % chips) * 2 + core
            target = (other // chips * chips + other % chips) * 2 + core
            pairs.append((source, target))
    return lax.ppermute(value, ("dp", "space"), pairs)


def sum_everywhere(mine, yours):
    odd = is_odd()
    dp_count, tm_count, space_count = (lax.axis_size(a) for a in ("dp", "tm", "space"))
    mine = mine + xor_permute(yours, "space", 1).astype(F32)
    members = dp_count * space_count // 2
    member = lax.axis_index("dp") * (space_count // 2) + lax.axis_index("space") // 2
    rows = mine.shape[0] // members
    sent = mine.astype(BF16)
    arrived = [
        plane_permute(take_rows(sent, member ^ mask, rows), mask, dp_count)
        for mask in range(1, members)
    ]
    chunk = take_rows(mine, member, rows)
    for piece in arrived:
        chunk = chunk + piece.astype(F32)
    chunk = chunk.astype(BF16)
    pieces = [chunk] + [xor_permute(chunk, "tm", mask) for mask in range(1, tm_count)]
    pieces = [piece.astype(F32) for piece in pieces]
    while len(pieces) > 1:
        pieces = [pieces[i] + pieces[i + 1] for i in range(0, len(pieces), 2)]
    chunk = pieces[0].astype(BF16)
    whole = jnp.zeros(mine.shape, BF16)
    whole = lax.dynamic_update_slice_in_dim(whole, chunk, member * rows, axis=0)
    for mask in range(1, members):
        whole = lax.dynamic_update_slice_in_dim(
            whole, plane_permute(chunk, mask, dp_count), (member ^ mask) * rows, axis=0
        )
    other = xor_permute(whole, "space", 1)
    return (
        jnp.where(odd, other, whole).astype(F32),
        jnp.where(odd, whole, other).astype(F32),
    )


def root_norm(values, gain):
    return values * lax.rsqrt(jnp.mean(values * values, axis=-1, keepdims=True) + 1e-06) * gain


def silu(values):
    return values * jax.nn.sigmoid(values)


def dot(left, right):
    return jnp.dot(left, right, preferred_element_type=F32)


def call(body, outs, specs, out_specs, scratch, flops, moved, *args):
    return pl.pallas_call(
        body,
        out_shape=outs,
        in_specs=specs,
        out_specs=out_specs,
        scratch_shapes=scratch,
        compiler_params=pltpu.CompilerParams(vmem_limit_bytes=LIMIT),
        cost_estimate=pl.CostEstimate(
            flops=int(flops), bytes_accessed=int(moved), transcendentals=0
        ),
    )(*(
        pltpu.with_memory_space_constraint(arg, pltpu.HBM) if spec is HBM else arg
        for arg, spec in zip(args, specs, strict=True)
    ))


def shape(rows, columns, dtype):
    return jax.ShapeDtypeStruct((rows, columns), dtype)


def is_odd():
    return lax.rem(lax.axis_index("space"), 2) == 1


def has_across():
    place = lax.axis_index("space")
    return jnp.logical_and(place > 0, place < lax.axis_size("space") - 1)


def choose_frames(pair, here):
    block = lax.axis_index("tm")
    low, high = pair[0][here], pair[1][here]
    chosen = jnp.where(lax.rem(block, 2) == 1, low, high)
    return jnp.where(block > 0, chosen, jnp.zeros_like(chosen))


def edge_rows(values, columns, odd):
    first, last = values[:columns], values[values.shape[0] - columns :]
    return jnp.where(odd, first, last), jnp.where(odd, last, first)


def norm_body(late, latent_hbm, gain_hbm, latent, normed_late, normed_early, gain, sems):
    frame_count, per_frame = latent_hbm.shape[:2]
    pltpu.make_async_copy(gain_hbm, gain, sems.at[frame_count]).start()
    copies = {}
    for frame in range(frame_count - 1, -1, -1):
        here = pl.ds(frame * per_frame, per_frame)
        copies[frame] = pltpu.make_async_copy(latent_hbm.at[frame], latent.at[here], sems.at[frame])
        copies[frame].start()
    pltpu.make_async_copy(gain_hbm, gain, sems.at[frame_count]).wait()
    for frame in range(frame_count - 1, -1, -1):
        copies[frame].wait()
        wide = latent[pl.ds(frame * per_frame, per_frame)].astype(F32)
        normed = root_norm(wide, gain[...].reshape(1, -1)).astype(BF16)
        at = frame - (frame_count - late)
        target = normed_late if at >= 0 else normed_early
        target[pl.ds((at if at >= 0 else frame) * per_frame, per_frame)] = normed


def prepare_body(
    latent, query_hbm, key_hbm, value_hbm, out_hbm, in_hbm, back_hbm, first_hbm, second_hbm,
    w_query, w_both, w_out, s_out, first, second, slope, hidden_t, latent_t, predicted,
    s_in, sems,
):
    channels = latent.shape[1]
    student = [
        pltpu.make_async_copy(in_hbm, s_in, sems.at[0]),
        pltpu.make_async_copy(back_hbm, s_out, sems.at[1]),
    ]
    rest = [
        pltpu.make_async_copy(query_hbm, w_query, sems.at[2]),
        pltpu.make_async_copy(key_hbm, w_both.at[:, pl.ds(0, channels)], sems.at[3]),
        pltpu.make_async_copy(value_hbm, w_both.at[:, pl.ds(channels, channels)], sems.at[4]),
        pltpu.make_async_copy(out_hbm, w_out, sems.at[5]),
    ]
    for at, (taps, packed) in enumerate(((first_hbm, first), (second_hbm, second))):
        for t in range(3):
            for r in range(3):
                for c in range(3):
                    block = packed.at[t, pl.ds(r * channels, channels), pl.ds(c * channels, channels)]
                    rest.append(
                        pltpu.make_async_copy(taps.at[t, r, c], block, sems.at[6 + 3 * at + t])
                    )
    for copy in student + rest:
        copy.start()
    tokens = latent[...]
    latent_t[...] = tokens.T
    student[0].wait()
    before = dot(tokens, s_in[...])
    hidden = silu(before).astype(BF16)
    logistic = jax.nn.sigmoid(before)
    slope[...] = logistic * (1.0 + before * (1.0 - logistic))
    hidden_t[...] = hidden.T
    student[1].wait()
    predicted[...] = tokens.astype(F32) + dot(hidden, s_out[...])
    for copy in rest:
        copy.wait()


def attend_body(blocks, start, count, later, columns, *refs):
    parts = refs[:blocks]
    latent, w_query, w_both, w_out, gain = refs[blocks : blocks + 5]
    act, mid, on, off = refs[-4:]
    channels = w_query.shape[0]
    odd = is_odd()
    per_frame = parts[0].shape[0] // count
    if later:
        for ends, others in zip((on, off), refs[blocks + 5 : -4], strict=True):
            ends[pl.ds(count * columns, others.shape[0])] = others[...]
    for frame in range(count - 1, -1, -1):
        here = pl.ds(frame * per_frame, per_frame)
        rows = jnp.concatenate([part[here] for part in parts], axis=0)
        queries = dot(parts[0][here], w_query[...]).astype(BF16)
        both = dot(rows, w_both[...]).astype(BF16)
        keys, values = both[:, :channels], both[:, channels:]
        scores = lax.dot_general(
            queries, keys, (((1,), (1,)), ((), ())), preferred_element_type=F32
        ) * channels ** (-0.5)
        expos = jnp.exp(scores - jnp.max(scores, axis=-1, keepdims=True))
        totals = jnp.sum(expos, axis=-1, keepdims=True)
        mixed = (dot(expos.astype(BF16), values) / totals).astype(BF16)
        own = latent[pl.ds((start + frame) * per_frame, per_frame)]
        middle = (own.astype(F32) + dot(mixed, w_out[...])).astype(BF16)
        mid[here] = middle
        active = silu(root_norm(middle.astype(F32), gain[...].reshape(1, -1))).astype(BF16)
        act[here] = active
        edge = pl.ds(frame * columns, columns)
        on[edge], off[edge] = edge_rows(active, columns, odd)


def stack_rows(columns, odd, own, on, off, stacked, at):
    per_frame, channels = own.shape
    base = at * per_frame
    split = per_frame - columns
    stacked[pl.ds(base, columns), 0:channels] = jnp.where(odd, on, off)
    stacked[pl.ds(base + columns, split), 0:channels] = own[:split]
    stacked[pl.ds(base, per_frame), channels : 2 * channels] = own
    stacked[pl.ds(base, split), 2 * channels :] = own[columns:]
    stacked[pl.ds(base + split, columns), 2 * channels :] = jnp.where(odd, off, on)


def taps_sum(sources, frame, stacked, packed, per_frame, total):
    for at, source in enumerate(sources):
        tap = source - frame
        if 0 <= tap < 3:
            term = dot(stacked[pl.ds(at * per_frame, per_frame)], packed[tap])
            total = term if total is None else total + term
    return total


def shift_columns(total, columns):
    rows, channels = total.shape[0], total.shape[1] // 3
    column = lax.broadcasted_iota(jnp.int32, (rows, channels), 0) % columns
    before = pltpu.roll(total[:, :channels], 1, 0)
    after = pltpu.roll(total[:, 2 * channels :], rows - 1, 0)
    return (
        total[:, channels : 2 * channels]
        + jnp.where(column == 0, 0.0, before)
        + jnp.where(column == columns - 1, 0.0, after)
    )


def own_body(groups, columns, *refs):
    odd = is_odd()
    far = has_across()
    off, on, packed, partial, stacked = refs[-5:]
    frame_count = sum(groups)
    per_frame = partial.shape[0] // frame_count
    at = 0
    for own, frames in zip(refs[:-5], groups, strict=True):
        for frame in range(frames):
            edge = pl.ds(at * columns, columns)
            stack_rows(
                columns, odd, own[pl.ds(frame * per_frame, per_frame)], on[edge],
                jnp.where(far, off[edge], jnp.zeros_like(off[edge])), stacked, at,
            )
            at += 1
    sources = range(2, frame_count + 2)
    for frame in range(frame_count):
        total = taps_sum(sources, frame, stacked, packed, per_frame, None)
        partial[pl.ds(frame * per_frame, per_frame)] = total


def earlier_body(columns, low, high, off, packed, partial, total, stacked):
    odd = is_odd()
    per_frame = stacked.shape[0] // 2
    for frame in range(2):
        tail = choose_frames((low, high), pl.ds(frame * per_frame, per_frame))
        edge = off[pl.ds(frame * columns, columns)]
        stack_rows(columns, odd, tail, jnp.zeros_like(edge), edge, stacked, frame)
    for frame in range(partial.shape[0] // per_frame):
        here = pl.ds(frame * per_frame, per_frame)
        total[here] = taps_sum((0, 1), frame, stacked, packed, per_frame, partial[here])


def partner_terms(columns, odd, pair, packed):
    per_frame = pair[0].shape[0] // 2
    channels = pair[0].shape[1]
    tap_row = pl.ds(pl.multiple_of(jnp.where(odd, 0, 2 * channels), channels), channels)
    edges = []
    for source in range(2):
        rows = choose_frames(pair, pl.ds(source * per_frame, per_frame))
        edges.append(edge_rows(rows, columns, jnp.logical_not(odd))[0])
    terms = []
    for frame in range(2):
        term = None
        for source in range(frame, 2):
            part = dot(edges[source], packed[source - frame, tap_row])
            term = part if term is None else term + part
        zeros = jnp.zeros_like(term)
        pieces = [jnp.where(odd, term, zeros), jnp.where(odd, zeros, term)]
        if per_frame > 2 * columns:
            pieces.insert(1, jnp.zeros((per_frame - 2 * columns, term.shape[1]), F32))
        terms.append(jnp.concatenate(pieces, axis=0))
    return terms


def first_body(
    columns, low, high, packed, partial, gain, act, late, on, off, off_late
):
    odd = is_odd()
    terms = partner_terms(columns, odd, (low, high), packed)
    per_frame = low.shape[0] // 2
    frame_count = partial.shape[0] // per_frame
    for frame in range(frame_count - 1, -1, -1):
        here = pl.ds(frame * per_frame, per_frame)
        total = partial[here]
        if frame < 2:
            total = total + terms[frame]
        total = shift_columns(total, columns)
        active = silu(root_norm(total, gain[...].reshape(1, -1))).astype(BF16)
        act[here] = active
        edge = pl.ds(frame * columns, columns)
        near, far = edge_rows(active, columns, odd)
        on[edge], off[edge] = near, far
        at = frame - (frame_count - 2)
        if at >= 0:
            late[pl.ds(at * per_frame, per_frame)] = active
            off_late[pl.ds(at * columns, columns)] = far


def last_body(
    columns, token_total, low, high, packed, partial, mid_early, mid_late,
    slope, hidden_t, latent_t, predicted, s_out, teacher, mine, yours, signals,
):
    odd = is_odd()
    terms = partner_terms(columns, odd, (low, high), packed)
    per_frame = low.shape[0] // 2
    frame_count = partial.shape[0] // per_frame
    for frame in range(frame_count - 1, -1, -1):
        here = pl.ds(frame * per_frame, per_frame)
        total = partial[here]
        if frame < 2:
            total = total + terms[frame]
        total = shift_columns(total, columns)
        at = frame - (frame_count - 2)
        mid = mid_late[pl.ds(at * per_frame, per_frame)] if at >= 0 else mid_early[here]
        taught = (mid.astype(F32) + total).astype(BF16)
        teacher[here] = taught
        error = predicted[here] - taught.astype(F32)
        signals[here] = (
            error * lax.rsqrt(error * error + 0.0625) * token_total ** (-0.5)
        ).astype(BF16)
    signal = signals[...]
    grad_out = dot(hidden_t[...], signal)
    back = lax.dot_general(
        signal, s_out[...], (((1,), (1,)), ((), ())), preferred_element_type=F32
    )
    back_pre = (back * slope[...]).astype(BF16)
    grad_in = dot(latent_t[...], back_pre)
    mine[...] = jnp.where(odd, grad_out, grad_in)
    yours[...] = jnp.where(odd, grad_in, grad_out).astype(BF16)


def shards(
    latent,
    attn_gain,
    w_query,
    w_key,
    w_value,
    w_out,
    conv_gain_first,
    conv_first,
    conv_gain_second,
    conv_second,
    student_in,
    student_out,
):
    frame_count, row_count, columns, channels = latent.shape[1:]
    per_frame = row_count * columns
    tokens = frame_count * per_frame
    early = frame_count - 2
    frames = latent.reshape(frame_count, per_frame, channels)
    unit = 2 * channels * channels
    square = shape(channels, channels, BF16)

    def rows_of(count):
        return shape(count * per_frame, channels, BF16)

    def edges_of(count):
        return shape(count * columns, channels, BF16)

    latent_rows, normed_late, normed_early = call(
        functools.partial(norm_body, 2),
        [rows_of(frame_count), rows_of(2), rows_of(early)], [HBM] * 2, [VMEM] * 3,
        [pltpu.VMEM((channels,), F32), pltpu.SemaphoreType.DMA((frame_count + 1,))],
        0, 4 * tokens * channels, frames, attn_gain,
    )
    blocks_late = gather_blocks(normed_late)
    blocks_early = gather_blocks(normed_early)

    packed_shape = jax.ShapeDtypeStruct((3, 3 * channels, 3 * channels), BF16)
    wide = shape(tokens, channels, F32)
    turned = shape(channels, tokens, BF16)
    weights = (w_query, w_key, w_value, w_out, student_in, student_out, conv_first, conv_second)
    (
        w_query, w_both, w_out, student_out, packed_first, packed_second,
        slope, hidden_t, latent_t, predicted,
    ) = call(
        prepare_body,
        [square, shape(channels, 2 * channels, BF16), square, square, packed_shape, packed_shape,
         wide, turned, turned, wide],
        [VMEM] + [HBM] * len(weights), [VMEM] * 10,
        [pltpu.VMEM((channels, channels), BF16), pltpu.SemaphoreType.DMA((12,))],
        2 * tokens * unit, 60 * channels * channels * 2, latent_rows, *weights,
    )

    def attend(blocks, start, count, *others):
        args = [*blocks, latent_rows, w_query, w_both, w_out, conv_gain_first, *others]
        ends = edges_of(count + 2 if others else count)
        return call(
            functools.partial(attend_body, len(blocks), start, count, bool(others), columns),
            [rows_of(count), rows_of(count), ends, ends],
            [VMEM] * len(args), [VMEM] * 4, [],
            (2 + 4 * len(blocks)) * count * per_frame * unit, 4 * count * per_frame * channels,
            *args,
        )

    def stacked(count):
        return pltpu.VMEM((count * per_frame, 3 * channels), BF16)

    def from_earlier(late, off):
        pair = frame_pairings(late)
        corner = across_next_frames(off)
        partner = [xor_permute(frames, "space", 1) for frames in pair]
        return pair, corner, partner

    def earlier_part(pair, corner, packed, partial):
        args = [*pair, corner, packed, partial]
        return call(
            functools.partial(earlier_body, columns),
            shape(tokens, 3 * channels, F32), [VMEM] * len(args), VMEM,
            [stacked(2)], 9 * tokens * unit, 8 * tokens * channels, *args,
        )

    def own_part(groups, on, off, packed):
        halo = [across_permute(off)]
        halo.append(xor_permute(on, "space", 1))
        args = [*(own for _, own in groups), *halo, packed]
        return call(
            functools.partial(own_body, [group[0] for group in groups], columns),
            shape(tokens, 3 * channels, F32), [VMEM] * len(args), VMEM,
            [stacked(frame_count)], 18 * tokens * unit, 8 * tokens * channels, *args,
        )

    act_late, mid_late, on_late, off_late = attend(blocks_late, early, 2)
    pair, corner, partner = from_earlier(act_late, off_late)
    act_early, mid_early, on, off = attend(blocks_early, 0, early, on_late, off_late)
    partial = own_part([(early, act_early), (2, act_late)], on, off, packed_first)
    partial = earlier_part(pair, corner, packed_first, partial)
    args = [*partner, packed_first, partial, conv_gain_second]
    act, late, on, off, off_late = call(
        functools.partial(first_body, columns),
        [rows_of(frame_count), rows_of(2), edges_of(frame_count), edges_of(frame_count), edges_of(2)],
        [VMEM] * len(args), [VMEM] * 5, [],
        9 * tokens * unit, 8 * tokens * channels, *args,
    )
    pair, corner, partner = from_earlier(late, off_late)
    partial = own_part([(frame_count, act)], on, off, packed_second)
    token_total = tokens * lax.axis_size("dp") * lax.axis_size("tm") * lax.axis_size("space")
    partial = earlier_part(pair, corner, packed_second, partial)
    args = [
        *partner, packed_second, partial, mid_early, mid_late,
        slope, hidden_t, latent_t, predicted, student_out,
    ]
    teacher, mine, yours = call(
        functools.partial(last_body, columns, token_total),
        [rows_of(frame_count), shape(channels, channels, F32), square],
        [VMEM] * len(args), [VMEM] * 3,
        [pltpu.VMEM((tokens, channels), BF16)],
        12 * tokens * unit, 8 * tokens * channels, *args,
    )
    grad_in, grad_out = sum_everywhere(mine, yours)
    return (teacher.reshape(latent.shape), grad_in, grad_out)


def solution(mesh):
    return jax.shard_map(
        shards,
        mesh=mesh,
        in_specs=(
            P("dp", "tm", "space", None, None),
            P(),
            P(),
            P(),
            P(),
            P(),
            P(),
            P(),
            P(),
            P(),
            P(),
            P(),
        ),
        out_specs=(P("dp", "tm", "space", None, None), P(), P()),
        check_vma=False,
    )
```

```python
import functools

import jax
import jax.numpy as jnp
from jax import lax
from jax.experimental import pallas as pl
from jax.experimental.pallas import tpu as pltpu
from jax.sharding import PartitionSpec as P


F32 = jnp.float32
BF16 = jnp.bfloat16
VMEM = pl.BlockSpec(memory_space=pltpu.VMEM)
HBM = pl.BlockSpec(memory_space=pltpu.HBM)
LIMIT = 20 << 20


def xor_permute(value, axis, mask):
    count = lax.axis_size(axis)
    return lax.ppermute(value, axis, [(i, i ^ mask) for i in range(count)])


def gather_chips(block):
    mask = lax.axis_size("space") // 2
    blocks = [block]
    while mask > 1:
        blocks = blocks + [xor_permute(b, "space", mask) for b in blocks]
        mask //= 2
    return blocks[1:]


def across_pairs():
    pairs = []
    for low in range(1, lax.axis_size("space") - 1, 2):
        pairs += [(low, low + 1), (low + 1, low)]
    return pairs


def across_permute(value):
    clips, count = lax.axis_size("dp"), lax.axis_size("space")
    rows = dict(across_pairs())
    pairs = []
    for clip in range(clips):
        for place in range(count):
            other = (clip, rows[place]) if place in rows else (clip ^ 1, place)
            if other[0] < clips:
                pairs.append((clip * count + place, other[0] * count + other[1]))
    return lax.ppermute(value, ("dp", "space"), pairs)


def frame_pairings(value):
    blocks, count = lax.axis_size("tm"), lax.axis_size("space")
    results = []
    for first in range(2):
        pairs = []
        for block in range(blocks):
            other = ((block - first) ^ 1) + first
            for place in range(count):
                inside = 0 <= other < blocks
                target = other * count + place if inside else block * count + (place ^ 1)
                pairs.append((block * count + place, target))
        results.append(lax.ppermute(value, ("tm", "space"), pairs))
    return results


def corner_pairings(value):
    clips, blocks, count = (lax.axis_size(axis) for axis in ("dp", "tm", "space"))
    rows = dict(across_pairs())
    results = []
    for first in range(2):
        pairs = []
        for clip in range(clips):
            for block in range(blocks):
                other = ((block - first) ^ 1) + first
                for place in range(count):
                    if place in rows and 0 <= other < blocks:
                        target = (clip * blocks + other) * count + rows[place]
                    else:
                        target = ((clip ^ 1) * blocks + block) * count + place
                    if target < clips * blocks * count:
                        pairs.append(((clip * blocks + block) * count + place, target))
        results.append(lax.ppermute(value, ("dp", "tm", "space"), pairs))
    return results


def take_rows(value, index, rows):
    return lax.dynamic_slice_in_dim(value, index * rows, rows, axis=0)


def plane_permute(value, mask, dp_count):
    chips = lax.axis_size("space") // 2
    pairs = []
    for member in range(dp_count * chips):
        other = member ^ mask
        for core in range(2):
            source = (member // chips * chips + member % chips) * 2 + core
            target = (other // chips * chips + other % chips) * 2 + core
            pairs.append((source, target))
    return lax.ppermute(value, ("dp", "space"), pairs)


def sum_everywhere(mine, yours):
    odd = is_odd()
    dp_count, tm_count, space_count = (lax.axis_size(a) for a in ("dp", "tm", "space"))
    mine = mine + xor_permute(yours, "space", 1).astype(F32)
    members = dp_count * space_count // 2
    member = lax.axis_index("dp") * (space_count // 2) + lax.axis_index("space") // 2
    rows = mine.shape[0] // members
    sent = mine.astype(BF16)
    arrived = [
        plane_permute(take_rows(sent, member ^ mask, rows), mask, dp_count)
        for mask in range(1, members)
    ]
    chunk = take_rows(mine, member, rows)
    for piece in arrived:
        chunk = chunk + piece.astype(F32)
    chunk = chunk.astype(BF16)
    pieces = [chunk] + [xor_permute(chunk, "tm", mask) for mask in range(1, tm_count)]
    pieces = [piece.astype(F32) for piece in pieces]
    while len(pieces) > 1:
        pieces = [pieces[i] + pieces[i + 1] for i in range(0, len(pieces), 2)]
    chunk = pieces[0].astype(BF16)
    whole = jnp.zeros(mine.shape, BF16)
    whole = lax.dynamic_update_slice_in_dim(whole, chunk, member * rows, axis=0)
    for mask in range(1, members):
        whole = lax.dynamic_update_slice_in_dim(
            whole, plane_permute(chunk, mask, dp_count), (member ^ mask) * rows, axis=0
        )
    other = xor_permute(whole, "space", 1)
    return (
        jnp.where(odd, other, whole).astype(F32),
        jnp.where(odd, whole, other).astype(F32),
    )


def root_norm(values, gain):
    return values * lax.rsqrt(jnp.mean(values * values, axis=-1, keepdims=True) + 1e-06) * gain


def silu(values):
    return values * jax.nn.sigmoid(values)


def dot(left, right):
    return jnp.dot(left, right, preferred_element_type=F32)


def call(body, outs, specs, out_specs, scratch, flops, moved, *args):
    return pl.pallas_call(
        body,
        out_shape=outs,
        in_specs=specs,
        out_specs=out_specs,
        scratch_shapes=scratch,
        compiler_params=pltpu.CompilerParams(vmem_limit_bytes=LIMIT),
        cost_estimate=pl.CostEstimate(
            flops=int(flops), bytes_accessed=int(moved), transcendentals=0
        ),
    )(*(
        pltpu.with_memory_space_constraint(arg, pltpu.HBM) if spec is HBM else arg
        for arg, spec in zip(args, specs, strict=True)
    ))


def shape(rows, columns, dtype):
    return jax.ShapeDtypeStruct((rows, columns), dtype)


def is_odd():
    return lax.rem(lax.axis_index("space"), 2) == 1


def has_across():
    place = lax.axis_index("space")
    return jnp.logical_and(place > 0, place < lax.axis_size("space") - 1)


def choose_frames(pair, here):
    block = lax.axis_index("tm")
    low, high = pair[0][here], pair[1][here]
    chosen = jnp.where(lax.rem(block, 2) == 1, low, high)
    return jnp.where(block > 0, chosen, jnp.zeros_like(chosen))


def edge_rows(values, columns, odd):
    first, last = values[:columns], values[values.shape[0] - columns :]
    return jnp.where(odd, first, last), jnp.where(odd, last, first)


def norm_body(latent_hbm, gain_hbm, latent, normed, *refs):
    frame_count, per_frame = latent_hbm.shape[:2]
    frames, gain, sems = refs[:frame_count], refs[-2], refs[-1]
    gain_copy = pltpu.make_async_copy(gain_hbm, gain, sems.at[frame_count])
    gain_copy.start()
    copies = {}
    for frame in range(frame_count - 1, -1, -1):
        here = pl.ds(frame * per_frame, per_frame)
        copies[frame] = pltpu.make_async_copy(latent_hbm.at[frame], latent.at[here], sems.at[frame])
        copies[frame].start()
    gain_copy.wait()
    for frame in range(frame_count - 1, -1, -1):
        here = pl.ds(frame * per_frame, per_frame)
        copies[frame].wait()
        wide = latent[here].astype(F32)
        result = root_norm(wide, gain[...].reshape(1, -1)).astype(BF16)
        normed[here] = result
        frames[frame][...] = result


def prepare_body(
    latent, normed, partner, query_hbm, key_hbm, value_hbm, out_hbm, in_hbm, back_hbm, first_hbm, second_hbm,
    w_both, w_out, s_out, first, second, slope, hidden_t, latent_t, predicted,
    queries, own_both, partner_both, w_query, s_in, sems,
):
    channels = latent.shape[1]
    early = [
        pltpu.make_async_copy(query_hbm, w_query, sems.at[2]),
        pltpu.make_async_copy(key_hbm, w_both.at[:, pl.ds(0, channels)], sems.at[3]),
        pltpu.make_async_copy(value_hbm, w_both.at[:, pl.ds(channels, channels)], sems.at[4]),
        pltpu.make_async_copy(in_hbm, s_in, sems.at[0]),
        pltpu.make_async_copy(back_hbm, s_out, sems.at[1]),
    ]
    rest = [pltpu.make_async_copy(out_hbm, w_out, sems.at[5])]
    for at, (taps, packed) in enumerate(((first_hbm, first), (second_hbm, second))):
        for t in range(3):
            for r in range(3):
                for c in range(3):
                    row = (3 * t + r) * channels
                    block = packed.at[pl.ds(row, channels), pl.ds(c * channels, channels)]
                    rest.append(
                        pltpu.make_async_copy(taps.at[t, r, c], block, sems.at[6 + 3 * at + t])
                    )
    for copy in early + rest:
        copy.start()
    tokens = latent[...]
    latent_t[...] = tokens.T
    early[0].wait()
    queries[...] = dot(normed[...], w_query[...]).astype(BF16)
    early[1].wait()
    early[2].wait()
    own_both[...] = dot(normed[...], w_both[...]).astype(BF16)
    partner_both[...] = dot(partner[...], w_both[...]).astype(BF16)
    early[3].wait()
    before = dot(tokens, s_in[...])
    hidden = silu(before).astype(BF16)
    logistic = jax.nn.sigmoid(before)
    slope[...] = logistic * (1.0 + before * (1.0 - logistic))
    hidden_t[...] = hidden.T
    early[4].wait()
    predicted[...] = tokens.astype(F32) + dot(hidden, s_out[...])
    for copy in rest:
        copy.wait()


def attend_body(frame, remote, columns, kept, *refs):
    blocks, refs = refs[:remote], refs[remote:]
    latent, queries, own_both, partner_both, w_both, w_out, gain = refs[:7]
    others, (act, mid, on, off) = refs[7 : 7 + kept], refs[7 + kept :]
    channels = w_out.shape[0]
    per_frame = mid.shape[0]
    odd = is_odd()
    for target, other in zip((on, off, act), others):
        rows = other.shape[0]
        target[pl.ds(target.shape[0] - rows, rows)] = other[...]
    here = pl.ds(frame * per_frame, per_frame)
    far = dot(jnp.concatenate([block[...] for block in blocks], axis=0), w_both[...]).astype(BF16)
    parts = [own_both[here], partner_both[here], far]
    keys = jnp.concatenate([part[:, :channels] for part in parts], axis=0)
    values = jnp.concatenate([part[:, channels:] for part in parts], axis=0)
    scores = lax.dot_general(
        queries[here], keys, (((1,), (1,)), ((), ())), preferred_element_type=F32
    ) * channels ** (-0.5)
    expos = jnp.exp(scores - jnp.max(scores, axis=-1, keepdims=True))
    totals = jnp.sum(expos, axis=-1, keepdims=True)
    mixed = (dot(expos.astype(BF16), values) / totals).astype(BF16)
    middle = (latent[here].astype(F32) + dot(mixed, w_out[...])).astype(BF16)
    mid[...] = middle
    active = silu(root_norm(middle.astype(F32), gain[...].reshape(1, -1))).astype(BF16)
    act[pl.ds(0, per_frame)] = active
    edge = pl.ds(0, columns)
    on[edge], off[edge] = edge_rows(active, columns, odd)


def stack_rows(columns, odd, own, on, off, stacked, at):
    per_frame, channels = own.shape
    base = at * per_frame
    split = per_frame - columns
    stacked[pl.ds(base, columns), 0:channels] = jnp.where(odd, on, off)
    stacked[pl.ds(base + columns, split), 0:channels] = own[:split]
    stacked[pl.ds(base, per_frame), channels : 2 * channels] = own
    stacked[pl.ds(base, split), 2 * channels :] = own[columns:]
    stacked[pl.ds(base + split, columns), 2 * channels :] = jnp.where(odd, off, on)


def taps_sum(sources, frame, stacked, packed, per_frame, total):
    at = [i for i, source in enumerate(sources) if 0 <= source - frame < 3]
    if not at:
        return total
    rows = [stacked[pl.ds(i * per_frame, per_frame)] for i in at]
    depth = stacked.shape[1]
    taps = packed[pl.ds((sources[at[0]] - frame) * depth, len(at) * depth)]
    term = dot(jnp.concatenate(rows, axis=1), taps)
    return term if total is None else total + term


def shift_columns(total, columns):
    rows, channels = total.shape[0], total.shape[1] // 3
    column = lax.broadcasted_iota(jnp.int32, (rows, channels), 0) % columns
    before = pltpu.roll(total[:, :channels], 1, 0)
    after = pltpu.roll(total[:, 2 * channels :], rows - 1, 0)
    return (
        total[:, channels : 2 * channels]
        + jnp.where(column == 0, 0.0, before)
        + jnp.where(column == columns - 1, 0.0, after)
    )


def own_body(groups, columns, *refs):
    odd = is_odd()
    far = has_across()
    off, on, packed, partial, stacked = refs[-5:]
    frame_count = sum(groups)
    per_frame = partial.shape[0] // frame_count
    at = 0
    for own, frames in zip(refs[:-5], groups, strict=True):
        for frame in range(frames):
            edge = pl.ds(at * columns, columns)
            stack_rows(
                columns, odd, own[pl.ds(frame * per_frame, per_frame)], on[edge],
                jnp.where(far, off[edge], jnp.zeros_like(off[edge])), stacked, at,
            )
            at += 1
    sources = range(2, frame_count + 2)
    for frame in range(frame_count):
        total = taps_sum(sources, frame, stacked, packed, per_frame, None)
        partial[pl.ds(frame * per_frame, per_frame)] = total


def earlier_body(columns, low, high, off_low, off_high, packed, partial, total, stacked):
    odd = is_odd()
    per_frame = stacked.shape[0] // 2
    for frame in range(2):
        tail = choose_frames((low, high), pl.ds(frame * per_frame, per_frame))
        edge = choose_frames((off_low, off_high), pl.ds(frame * columns, columns))
        edge = jnp.where(has_across(), edge, jnp.zeros_like(edge))
        stack_rows(columns, odd, tail, jnp.zeros_like(edge), edge, stacked, frame)
    for frame in range(partial.shape[0] // per_frame):
        here = pl.ds(frame * per_frame, per_frame)
        total[here] = taps_sum((0, 1), frame, stacked, packed, per_frame, partial[here])


def partner_terms(columns, odd, pair, packed):
    per_frame = pair[0].shape[0] // 2
    channels = pair[0].shape[1]
    row = jnp.where(odd, 0, 2 * channels)
    edges = []
    for source in range(2):
        rows = choose_frames(pair, pl.ds(source * per_frame, per_frame))
        edges.append(edge_rows(rows, columns, jnp.logical_not(odd))[0])
    terms = []
    for frame in range(2):
        term = None
        for source in range(frame, 2):
            start = pl.multiple_of(3 * (source - frame) * channels + row, channels)
            part = dot(edges[source], packed[pl.ds(start, channels)])
            term = part if term is None else term + part
        zeros = jnp.zeros_like(term)
        pieces = [jnp.where(odd, term, zeros), jnp.where(odd, zeros, term)]
        if per_frame > 2 * columns:
            pieces.insert(1, jnp.zeros((per_frame - 2 * columns, term.shape[1]), F32))
        terms.append(jnp.concatenate(pieces, axis=0))
    return terms


def first_body(
    columns, low, high, packed, partial, gain, act, late, on, off, off_late
):
    odd = is_odd()
    terms = partner_terms(columns, odd, (low, high), packed)
    per_frame = low.shape[0] // 2
    frame_count = partial.shape[0] // per_frame
    for frame in range(frame_count - 1, -1, -1):
        here = pl.ds(frame * per_frame, per_frame)
        total = partial[here]
        if frame < 2:
            total = total + terms[frame]
        total = shift_columns(total, columns)
        active = silu(root_norm(total, gain[...].reshape(1, -1))).astype(BF16)
        act[here] = active
        edge = pl.ds(frame * columns, columns)
        near, far = edge_rows(active, columns, odd)
        on[edge], off[edge] = near, far
        at = frame - (frame_count - 2)
        if at >= 0:
            late[pl.ds(at * per_frame, per_frame)] = active
            off_late[pl.ds(at * columns, columns)] = far


def last_body(columns, token_total, low, high, packed, partial, *refs):
    slope, hidden_t, latent_t, predicted, s_out, teacher, mine, yours, signals = refs[-9:]
    mids = refs[:-9]
    odd = is_odd()
    terms = partner_terms(columns, odd, (low, high), packed)
    per_frame = low.shape[0] // 2
    frame_count = partial.shape[0] // per_frame
    for frame in range(frame_count - 1, -1, -1):
        here = pl.ds(frame * per_frame, per_frame)
        total = partial[here]
        if frame < 2:
            total = total + terms[frame]
        total = shift_columns(total, columns)
        taught = (mids[frame][...].astype(F32) + total).astype(BF16)
        teacher[here] = taught
        error = predicted[here] - taught.astype(F32)
        signals[here] = (
            error * lax.rsqrt(error * error + 0.0625) * token_total ** (-0.5)
        ).astype(BF16)
    signal = signals[...]
    grad_out = dot(hidden_t[...], signal)
    back = lax.dot_general(
        signal, s_out[...], (((1,), (1,)), ((), ())), preferred_element_type=F32
    )
    back_pre = (back * slope[...]).astype(BF16)
    grad_in = dot(latent_t[...], back_pre)
    mine[...] = jnp.where(odd, grad_out, grad_in)
    yours[...] = jnp.where(odd, grad_in, grad_out).astype(BF16)


def shards(
    latent,
    attn_gain,
    w_query,
    w_key,
    w_value,
    w_out,
    conv_gain_first,
    conv_first,
    conv_gain_second,
    conv_second,
    student_in,
    student_out,
):
    frame_count, row_count, columns, channels = latent.shape[1:]
    per_frame = row_count * columns
    tokens = frame_count * per_frame
    early = frame_count - 2
    frames = latent.reshape(frame_count, per_frame, channels)
    unit = 2 * channels * channels
    square = shape(channels, channels, BF16)

    def rows_of(count):
        return shape(count * per_frame, channels, BF16)

    def edges_of(count):
        return shape(count * columns, channels, BF16)

    latent_rows, normed, *singles = call(
        norm_body,
        [rows_of(frame_count), rows_of(frame_count)] + [rows_of(1)] * frame_count,
        [HBM] * 2, [VMEM] * (2 + frame_count),
        [pltpu.VMEM((channels,), F32), pltpu.SemaphoreType.DMA((frame_count + 1,))],
        0, 4 * tokens * channels, frames, attn_gain,
    )
    order = list(range(frame_count - 1, -1, -1))
    gathered = {frame: gather_chips(singles[frame]) for frame in order}

    packed_shape = shape(9 * channels, 3 * channels, BF16)
    wide = shape(tokens, channels, F32)
    turned = shape(channels, tokens, BF16)
    both = shape(tokens, 2 * channels, BF16)
    weights = (w_query, w_key, w_value, w_out, student_in, student_out, conv_first, conv_second)
    (
        w_both, w_out, student_out, packed_first, packed_second,
        slope, hidden_t, latent_t, predicted, queries, own_both, partner_both,
    ) = call(
        prepare_body,
        [shape(channels, 2 * channels, BF16), square, square, packed_shape, packed_shape,
         wide, turned, turned, wide, rows_of(frame_count), both, both],
        [VMEM] * 3 + [HBM] * len(weights), [VMEM] * 12,
        [pltpu.VMEM((channels, channels), BF16)] * 2 + [pltpu.SemaphoreType.DMA((12,))],
        7 * tokens * unit, 60 * channels * channels * 2,
        latent_rows, normed, xor_permute(normed, "space", 1), *weights,
    )

    acts, mids, others = {}, {}, ()
    for turn, frame in enumerate(order):
        chips = gathered[frame]
        blocks = [*chips, *(xor_permute(block, "space", 1) for block in chips)]
        args = [
            *blocks, latent_rows, queries, own_both, partner_both, w_both, w_out,
            conv_gain_first, *others,
        ]
        ends = edges_of(turn + 1)
        acts[frame], mids[frame], on, off = call(
            functools.partial(attend_body, frame, len(blocks), columns, len(others)),
            [rows_of(2 if turn == 1 else 1), rows_of(1), ends, ends],
            [VMEM] * len(args), [VMEM] * 4, [],
            (4 + 2 * len(blocks)) * per_frame * unit, 4 * per_frame * channels, *args,
        )
        others = (on, off, acts[frame]) if turn == 0 else (on, off)
        if turn == 1:
            late, off_late = acts[frame], off

    def stacked(count):
        return pltpu.VMEM((count * per_frame, 3 * channels), BF16)

    def from_earlier(late, off):
        pair = frame_pairings(late)
        corner = corner_pairings(off)
        partner = [xor_permute(frames, "space", 1) for frames in pair]
        return pair, corner, partner

    def earlier_part(pair, corner, packed, partial):
        args = [*pair, *corner, packed, partial]
        return call(
            functools.partial(earlier_body, columns),
            shape(tokens, 3 * channels, F32), [VMEM] * len(args), VMEM,
            [stacked(2)], 9 * tokens * unit, 8 * tokens * channels, *args,
        )

    def own_part(groups, on, off, packed):
        halo = [across_permute(off)]
        halo.append(xor_permute(on, "space", 1))
        args = [*(own for _, own in groups), *halo, packed]
        return call(
            functools.partial(own_body, [group[0] for group in groups], columns),
            shape(tokens, 3 * channels, F32), [VMEM] * len(args), VMEM,
            [stacked(frame_count)], 18 * tokens * unit, 8 * tokens * channels, *args,
        )

    pair, corner, partner = from_earlier(late, off_late)
    groups = [(1, acts[frame]) for frame in range(early)] + [(2, late)]
    partial = own_part(groups, on, off, packed_first)
    partial = earlier_part(pair, corner, packed_first, partial)
    args = [*partner, packed_first, partial, conv_gain_second]
    act, late, on, off, off_late = call(
        functools.partial(first_body, columns),
        [rows_of(frame_count), rows_of(2), edges_of(frame_count), edges_of(frame_count), edges_of(2)],
        [VMEM] * len(args), [VMEM] * 5, [],
        9 * tokens * unit, 8 * tokens * channels, *args,
    )
    pair, corner, partner = from_earlier(late, off_late)
    partial = own_part([(frame_count, act)], on, off, packed_second)
    token_total = tokens * lax.axis_size("dp") * lax.axis_size("tm") * lax.axis_size("space")
    partial = earlier_part(pair, corner, packed_second, partial)
    args = [
        *partner, packed_second, partial, *(mids[frame] for frame in range(frame_count)),
        slope, hidden_t, latent_t, predicted, student_out,
    ]
    teacher, mine, yours = call(
        functools.partial(last_body, columns, token_total),
        [rows_of(frame_count), shape(channels, channels, F32), square],
        [VMEM] * len(args), [VMEM] * 3,
        [pltpu.VMEM((tokens, channels), BF16)],
        12 * tokens * unit, 8 * tokens * channels, *args,
    )
    grad_in, grad_out = sum_everywhere(mine, yours)
    return (teacher.reshape(latent.shape), grad_in, grad_out)


def solution(mesh):
    return jax.shard_map(
        shards,
        mesh=mesh,
        in_specs=(
            P("dp", "tm", "space", None, None),
            P(),
            P(),
            P(),
            P(),
            P(),
            P(),
            P(),
            P(),
            P(),
            P(),
            P(),
        ),
        out_specs=(P("dp", "tm", "space", None, None), P(), P()),
        check_vma=False,
    )
```

```python
import functools

import jax
import jax.numpy as jnp
from jax import lax
from jax.experimental import pallas as pl
from jax.experimental.pallas import tpu as pltpu
from jax.sharding import PartitionSpec as P


F32 = jnp.float32
BF16 = jnp.bfloat16
VMEM = pl.BlockSpec(memory_space=pltpu.VMEM)
HBM = pl.BlockSpec(memory_space=pltpu.HBM)
LIMIT = 20 << 20


def xor_permute(value, axis, mask):
    count = lax.axis_size(axis)
    return lax.ppermute(value, axis, [(i, i ^ mask) for i in range(count)])


def gather_chips(block):
    mask = lax.axis_size("space") // 2
    blocks = [block]
    while mask > 1:
        blocks = blocks + [xor_permute(b, "space", mask) for b in blocks]
        mask //= 2
    return blocks[1:]


def across_pairs():
    pairs = []
    for low in range(1, lax.axis_size("space") - 1, 2):
        pairs += [(low, low + 1), (low + 1, low)]
    return pairs


def across_permute(value):
    clips, count = lax.axis_size("dp"), lax.axis_size("space")
    rows = dict(across_pairs())
    pairs = []
    for clip in range(clips):
        for place in range(count):
            other = (clip, rows[place]) if place in rows else (clip ^ 1, place)
            if other[0] < clips:
                pairs.append((clip * count + place, other[0] * count + other[1]))
    return lax.ppermute(value, ("dp", "space"), pairs)


def frame_pairings(value):
    blocks, count = lax.axis_size("tm"), lax.axis_size("space")
    results = []
    for first in range(2):
        pairs = []
        for block in range(blocks):
            other = ((block - first) ^ 1) + first
            for place in range(count):
                inside = 0 <= other < blocks
                target = other * count + place if inside else block * count + (place ^ 1)
                pairs.append((block * count + place, target))
        results.append(lax.ppermute(value, ("tm", "space"), pairs))
    return results


def across_next_frames(value):
    count = lax.axis_size("space")
    pairs = [
        (block * count + source, (block + 1) * count + target)
        for block in range(lax.axis_size("tm") - 1)
        for source, target in across_pairs()
    ]
    return lax.ppermute(value, ("tm", "space"), pairs)


def take_rows(value, index, rows):
    return lax.dynamic_slice_in_dim(value, index * rows, rows, axis=0)


def plane_permute(value, mask, dp_count):
    chips = lax.axis_size("space") // 2
    pairs = []
    for member in range(dp_count * chips):
        other = member ^ mask
        for core in range(2):
            source = (member // chips * chips + member % chips) * 2 + core
            target = (other // chips * chips + other % chips) * 2 + core
            pairs.append((source, target))
    return lax.ppermute(value, ("dp", "space"), pairs)


def span_permute(value, mask):
    return xor_permute(value, "tm", mask)


def sum_everywhere(mine, yours):
    odd = is_odd()
    dp_count, tm_count, space_count = (lax.axis_size(a) for a in ("dp", "tm", "space"))
    mine = mine + xor_permute(yours, "space", 1).astype(F32)
    members = dp_count * space_count // 2
    member = lax.axis_index("dp") * (space_count // 2) + lax.axis_index("space") // 2
    rows = mine.shape[0] // members
    sent = mine.astype(BF16)
    arrived = [
        plane_permute(take_rows(sent, member ^ mask, rows), mask, dp_count)
        for mask in range(1, members)
    ]
    chunk = take_rows(mine, member, rows)
    for piece in arrived:
        chunk = chunk + piece.astype(F32)
    chunk = chunk.astype(BF16)
    pieces = [chunk] + [span_permute(chunk, mask) for mask in range(1, tm_count)]
    pieces = [piece.astype(F32) for piece in pieces]
    while len(pieces) > 1:
        pieces = [pieces[i] + pieces[i + 1] for i in range(0, len(pieces), 2)]
    chunk = pieces[0].astype(BF16)
    whole = jnp.zeros(mine.shape, BF16)
    whole = lax.dynamic_update_slice_in_dim(whole, chunk, member * rows, axis=0)
    for mask in range(1, members):
        whole = lax.dynamic_update_slice_in_dim(
            whole, plane_permute(chunk, mask, dp_count), (member ^ mask) * rows, axis=0
        )
    other = xor_permute(whole, "space", 1)
    return (
        jnp.where(odd, other, whole).astype(F32),
        jnp.where(odd, whole, other).astype(F32),
    )


def root_norm(values, gain):
    return values * lax.rsqrt(jnp.mean(values * values, axis=-1, keepdims=True) + 1e-06) * gain


def silu(values):
    return values * jax.nn.sigmoid(values)


def dot(left, right):
    return jnp.dot(left, right, preferred_element_type=F32)


def call(body, outs, specs, out_specs, scratch, flops, moved, *args):
    return pl.pallas_call(
        body,
        out_shape=outs,
        in_specs=specs,
        out_specs=out_specs,
        scratch_shapes=scratch,
        compiler_params=pltpu.CompilerParams(vmem_limit_bytes=LIMIT),
        cost_estimate=pl.CostEstimate(
            flops=int(flops), bytes_accessed=int(moved), transcendentals=0
        ),
    )(*(
        pltpu.with_memory_space_constraint(arg, pltpu.HBM) if spec is HBM else arg
        for arg, spec in zip(args, specs, strict=True)
    ))


def shape(rows, columns, dtype):
    return jax.ShapeDtypeStruct((rows, columns), dtype)


def is_odd():
    return lax.rem(lax.axis_index("space"), 2) == 1


def has_across():
    place = lax.axis_index("space")
    return jnp.logical_and(place > 0, place < lax.axis_size("space") - 1)


def choose_frames(pair, here):
    block = lax.axis_index("tm")
    low, high = pair[0][here], pair[1][here]
    chosen = jnp.where(lax.rem(block, 2) == 1, low, high)
    return jnp.where(block > 0, chosen, jnp.zeros_like(chosen))


def edge_rows(values, columns, odd):
    first, last = values[:columns], values[values.shape[0] - columns :]
    return jnp.where(odd, first, last), jnp.where(odd, last, first)


def norm_body(latent_hbm, gain_hbm, latent, normed, *refs):
    frame_count, per_frame = latent_hbm.shape[:2]
    frames, gain, sems = refs[:frame_count], refs[-2], refs[-1]
    gain_copy = pltpu.make_async_copy(gain_hbm, gain, sems.at[frame_count])
    gain_copy.start()
    copies = {}
    for frame in range(frame_count - 1, -1, -1):
        here = pl.ds(frame * per_frame, per_frame)
        copies[frame] = pltpu.make_async_copy(latent_hbm.at[frame], latent.at[here], sems.at[frame])
        copies[frame].start()
    gain_copy.wait()
    for frame in range(frame_count - 1, -1, -1):
        here = pl.ds(frame * per_frame, per_frame)
        copies[frame].wait()
        wide = latent[here].astype(F32)
        result = root_norm(wide, gain[...].reshape(1, -1)).astype(BF16)
        normed[here] = result
        frames[frame][...] = result


def prepare_body(
    latent, normed, partner, query_hbm, key_hbm, value_hbm, out_hbm, in_hbm, back_hbm, first_hbm, second_hbm,
    w_both, w_out, s_out, first, second, slope, hidden_t, latent_t, predicted,
    queries, own_both, partner_both, w_query, s_in, sems,
):
    channels = latent.shape[1]
    early = [
        pltpu.make_async_copy(query_hbm, w_query, sems.at[2]),
        pltpu.make_async_copy(key_hbm, w_both.at[:, pl.ds(0, channels)], sems.at[3]),
        pltpu.make_async_copy(value_hbm, w_both.at[:, pl.ds(channels, channels)], sems.at[4]),
        pltpu.make_async_copy(in_hbm, s_in, sems.at[0]),
        pltpu.make_async_copy(back_hbm, s_out, sems.at[1]),
    ]
    rest = [pltpu.make_async_copy(out_hbm, w_out, sems.at[5])]
    for at, (taps, packed) in enumerate(((first_hbm, first), (second_hbm, second))):
        for t in range(3):
            for r in range(3):
                for c in range(3):
                    row = (3 * t + r) * channels
                    block = packed.at[pl.ds(row, channels), pl.ds(c * channels, channels)]
                    rest.append(
                        pltpu.make_async_copy(taps.at[t, r, c], block, sems.at[6 + 3 * at + t])
                    )
    for copy in early + rest:
        copy.start()
    tokens = latent[...]
    latent_t[...] = tokens.T
    early[0].wait()
    queries[...] = dot(normed[...], w_query[...]).astype(BF16)
    early[1].wait()
    early[2].wait()
    own_both[...] = dot(normed[...], w_both[...]).astype(BF16)
    partner_both[...] = dot(partner[...], w_both[...]).astype(BF16)
    early[3].wait()
    before = dot(tokens, s_in[...])
    hidden = silu(before).astype(BF16)
    logistic = jax.nn.sigmoid(before)
    slope[...] = logistic * (1.0 + before * (1.0 - logistic))
    hidden_t[...] = hidden.T
    early[4].wait()
    predicted[...] = tokens.astype(F32) + dot(hidden, s_out[...])
    for copy in rest:
        copy.wait()


def attend_body(frame, remote, columns, kept, *refs):
    blocks, refs = refs[:remote], refs[remote:]
    latent, queries, own_both, partner_both, w_both, w_out, gain = refs[:7]
    others, (act, mid, on, off) = refs[7 : 7 + kept], refs[7 + kept :]
    channels = w_out.shape[0]
    per_frame = mid.shape[0]
    odd = is_odd()
    for target, other in zip((on, off, act), others):
        rows = other.shape[0]
        target[pl.ds(target.shape[0] - rows, rows)] = other[...]
    here = pl.ds(frame * per_frame, per_frame)
    far = dot(jnp.concatenate([block[...] for block in blocks], axis=0), w_both[...]).astype(BF16)
    parts = [own_both[here], partner_both[here], far]
    keys = jnp.concatenate([part[:, :channels] for part in parts], axis=0)
    values = jnp.concatenate([part[:, channels:] for part in parts], axis=0)
    scores = lax.dot_general(
        queries[here], keys, (((1,), (1,)), ((), ())), preferred_element_type=F32
    ) * channels ** (-0.5)
    expos = jnp.exp(scores - jnp.max(scores, axis=-1, keepdims=True))
    totals = jnp.sum(expos, axis=-1, keepdims=True)
    mixed = (dot(expos.astype(BF16), values) / totals).astype(BF16)
    middle = (latent[here].astype(F32) + dot(mixed, w_out[...])).astype(BF16)
    mid[...] = middle
    active = silu(root_norm(middle.astype(F32), gain[...].reshape(1, -1))).astype(BF16)
    act[pl.ds(0, per_frame)] = active
    edge = pl.ds(0, columns)
    on[edge], off[edge] = edge_rows(active, columns, odd)


def stack_rows(columns, odd, own, on, off, stacked, at):
    per_frame, channels = own.shape
    base = at * per_frame
    split = per_frame - columns
    stacked[pl.ds(base, columns), 0:channels] = jnp.where(odd, on, off)
    stacked[pl.ds(base + columns, split), 0:channels] = own[:split]
    stacked[pl.ds(base, per_frame), channels : 2 * channels] = own
    stacked[pl.ds(base, split), 2 * channels :] = own[columns:]
    stacked[pl.ds(base + split, columns), 2 * channels :] = jnp.where(odd, off, on)


def taps_sum(sources, frame, stacked, packed, per_frame, total):
    at = [i for i, source in enumerate(sources) if 0 <= source - frame < 3]
    if not at:
        return total
    rows = [stacked[pl.ds(i * per_frame, per_frame)] for i in at]
    depth = stacked.shape[1]
    taps = packed[pl.ds((sources[at[0]] - frame) * depth, len(at) * depth)]
    term = dot(jnp.concatenate(rows, axis=1), taps)
    return term if total is None else total + term


def shift_columns(total, columns):
    rows, channels = total.shape[0], total.shape[1] // 3
    column = lax.broadcasted_iota(jnp.int32, (rows, channels), 0) % columns
    before = pltpu.roll(total[:, :channels], 1, 0)
    after = pltpu.roll(total[:, 2 * channels :], rows - 1, 0)
    return (
        total[:, channels : 2 * channels]
        + jnp.where(column == 0, 0.0, before)
        + jnp.where(column == columns - 1, 0.0, after)
    )


def own_body(groups, columns, *refs):
    odd = is_odd()
    far = has_across()
    off, on, packed, partial, stacked = refs[-5:]
    frame_count = sum(groups)
    per_frame = partial.shape[0] // frame_count
    at = 0
    for own, frames in zip(refs[:-5], groups, strict=True):
        for frame in range(frames):
            edge = pl.ds(at * columns, columns)
            stack_rows(
                columns, odd, own[pl.ds(frame * per_frame, per_frame)], on[edge],
                jnp.where(far, off[edge], jnp.zeros_like(off[edge])), stacked, at,
            )
            at += 1
    sources = range(2, frame_count + 2)
    for frame in range(frame_count):
        total = taps_sum(sources, frame, stacked, packed, per_frame, None)
        partial[pl.ds(frame * per_frame, per_frame)] = total


def earlier_body(columns, low, high, off, packed, partial, total, stacked):
    odd = is_odd()
    per_frame = stacked.shape[0] // 2
    for frame in range(2):
        tail = choose_frames((low, high), pl.ds(frame * per_frame, per_frame))
        edge = off[pl.ds(frame * columns, columns)]
        stack_rows(columns, odd, tail, jnp.zeros_like(edge), edge, stacked, frame)
    for frame in range(partial.shape[0] // per_frame):
        here = pl.ds(frame * per_frame, per_frame)
        total[here] = taps_sum((0, 1), frame, stacked, packed, per_frame, partial[here])


def partner_terms(columns, odd, pair, packed):
    per_frame = pair[0].shape[0] // 2
    channels = pair[0].shape[1]
    row = jnp.where(odd, 0, 2 * channels)
    edges = []
    for source in range(2):
        rows = choose_frames(pair, pl.ds(source * per_frame, per_frame))
        edges.append(edge_rows(rows, columns, jnp.logical_not(odd))[0])
    terms = []
    for frame in range(2):
        term = None
        for source in range(frame, 2):
            start = pl.multiple_of(3 * (source - frame) * channels + row, channels)
            part = dot(edges[source], packed[pl.ds(start, channels)])
            term = part if term is None else term + part
        zeros = jnp.zeros_like(term)
        pieces = [jnp.where(odd, term, zeros), jnp.where(odd, zeros, term)]
        if per_frame > 2 * columns:
            pieces.insert(1, jnp.zeros((per_frame - 2 * columns, term.shape[1]), F32))
        terms.append(jnp.concatenate(pieces, axis=0))
    return terms


def first_body(
    columns, low, high, packed, partial, gain, act, late, on, off, off_late
):
    odd = is_odd()
    terms = partner_terms(columns, odd, (low, high), packed)
    per_frame = low.shape[0] // 2
    frame_count = partial.shape[0] // per_frame
    for frame in range(frame_count - 1, -1, -1):
        here = pl.ds(frame * per_frame, per_frame)
        total = partial[here]
        if frame < 2:
            total = total + terms[frame]
        total = shift_columns(total, columns)
        active = silu(root_norm(total, gain[...].reshape(1, -1))).astype(BF16)
        act[here] = active
        edge = pl.ds(frame * columns, columns)
        near, far = edge_rows(active, columns, odd)
        on[edge], off[edge] = near, far
        at = frame - (frame_count - 2)
        if at >= 0:
            late[pl.ds(at * per_frame, per_frame)] = active
            off_late[pl.ds(at * columns, columns)] = far


def last_body(columns, token_total, low, high, packed, partial, *refs):
    slope, hidden_t, latent_t, predicted, s_out, teacher, mine, yours, signals = refs[-9:]
    mids = refs[:-9]
    odd = is_odd()
    terms = partner_terms(columns, odd, (low, high), packed)
    per_frame = low.shape[0] // 2
    frame_count = partial.shape[0] // per_frame
    for frame in range(frame_count - 1, -1, -1):
        here = pl.ds(frame * per_frame, per_frame)
        total = partial[here]
        if frame < 2:
            total = total + terms[frame]
        total = shift_columns(total, columns)
        taught = (mids[frame][...].astype(F32) + total).astype(BF16)
        teacher[here] = taught
        error = predicted[here] - taught.astype(F32)
        signals[here] = (
            error * lax.rsqrt(error * error + 0.0625) * token_total ** (-0.5)
        ).astype(BF16)
    signal = signals[...]
    grad_out = dot(hidden_t[...], signal)
    back = lax.dot_general(
        signal, s_out[...], (((1,), (1,)), ((), ())), preferred_element_type=F32
    )
    back_pre = (back * slope[...]).astype(BF16)
    grad_in = dot(latent_t[...], back_pre)
    mine[...] = jnp.where(odd, grad_out, grad_in)
    yours[...] = jnp.where(odd, grad_in, grad_out).astype(BF16)


def shards(
    latent,
    attn_gain,
    w_query,
    w_key,
    w_value,
    w_out,
    conv_gain_first,
    conv_first,
    conv_gain_second,
    conv_second,
    student_in,
    student_out,
):
    frame_count, row_count, columns, channels = latent.shape[1:]
    per_frame = row_count * columns
    tokens = frame_count * per_frame
    early = frame_count - 2
    frames = latent.reshape(frame_count, per_frame, channels)
    unit = 2 * channels * channels
    square = shape(channels, channels, BF16)

    def rows_of(count):
        return shape(count * per_frame, channels, BF16)

    def edges_of(count):
        return shape(count * columns, channels, BF16)

    latent_rows, normed, *singles = call(
        norm_body,
        [rows_of(frame_count), rows_of(frame_count)] + [rows_of(1)] * frame_count,
        [HBM] * 2, [VMEM] * (2 + frame_count),
        [pltpu.VMEM((channels,), F32), pltpu.SemaphoreType.DMA((frame_count + 1,))],
        0, 4 * tokens * channels, frames, attn_gain,
    )
    order = list(range(frame_count - 1, -1, -1))
    gathered = {frame: gather_chips(singles[frame]) for frame in order}

    packed_shape = shape(9 * channels, 3 * channels, BF16)
    wide = shape(tokens, channels, F32)
    turned = shape(channels, tokens, BF16)
    both = shape(tokens, 2 * channels, BF16)
    weights = (w_query, w_key, w_value, w_out, student_in, student_out, conv_first, conv_second)
    (
        w_both, w_out, student_out, packed_first, packed_second,
        slope, hidden_t, latent_t, predicted, queries, own_both, partner_both,
    ) = call(
        prepare_body,
        [shape(channels, 2 * channels, BF16), square, square, packed_shape, packed_shape,
         wide, turned, turned, wide, rows_of(frame_count), both, both],
        [VMEM] * 3 + [HBM] * len(weights), [VMEM] * 12,
        [pltpu.VMEM((channels, channels), BF16)] * 2 + [pltpu.SemaphoreType.DMA((12,))],
        7 * tokens * unit, 60 * channels * channels * 2,
        latent_rows, normed, xor_permute(normed, "space", 1), *weights,
    )

    acts, mids, others = {}, {}, ()
    for turn, frame in enumerate(order):
        chips = gathered[frame]
        blocks = [*chips, *(xor_permute(block, "space", 1) for block in chips)]
        args = [
            *blocks, latent_rows, queries, own_both, partner_both, w_both, w_out,
            conv_gain_first, *others,
        ]
        ends = edges_of(turn + 1)
        acts[frame], mids[frame], on, off = call(
            functools.partial(attend_body, frame, len(blocks), columns, len(others)),
            [rows_of(2 if turn == 1 else 1), rows_of(1), ends, ends],
            [VMEM] * len(args), [VMEM] * 4, [],
            (4 + 2 * len(blocks)) * per_frame * unit, 4 * per_frame * channels, *args,
        )
        others = (on, off, acts[frame]) if turn == 0 else (on, off)
        if turn == 1:
            late, off_late = acts[frame], off

    def stacked(count):
        return pltpu.VMEM((count * per_frame, 3 * channels), BF16)

    def from_earlier(late, off):
        pair = frame_pairings(late)
        corner = across_next_frames(off)
        partner = [xor_permute(frames, "space", 1) for frames in pair]
        return pair, corner, partner

    def earlier_part(pair, corner, packed, partial):
        args = [*pair, corner, packed, partial]
        return call(
            functools.partial(earlier_body, columns),
            shape(tokens, 3 * channels, F32), [VMEM] * len(args), VMEM,
            [stacked(2)], 9 * tokens * unit, 8 * tokens * channels, *args,
        )

    def own_part(groups, on, off, packed):
        halo = [across_permute(off)]
        halo.append(xor_permute(on, "space", 1))
        args = [*(own for _, own in groups), *halo, packed]
        return call(
            functools.partial(own_body, [group[0] for group in groups], columns),
            shape(tokens, 3 * channels, F32), [VMEM] * len(args), VMEM,
            [stacked(frame_count)], 18 * tokens * unit, 8 * tokens * channels, *args,
        )

    pair, corner, partner = from_earlier(late, off_late)
    groups = [(1, acts[frame]) for frame in range(early)] + [(2, late)]
    partial = own_part(groups, on, off, packed_first)
    partial = earlier_part(pair, corner, packed_first, partial)
    args = [*partner, packed_first, partial, conv_gain_second]
    act, late, on, off, off_late = call(
        functools.partial(first_body, columns),
        [rows_of(frame_count), rows_of(2), edges_of(frame_count), edges_of(frame_count), edges_of(2)],
        [VMEM] * len(args), [VMEM] * 5, [],
        9 * tokens * unit, 8 * tokens * channels, *args,
    )
    pair, corner, partner = from_earlier(late, off_late)
    partial = own_part([(frame_count, act)], on, off, packed_second)
    token_total = tokens * lax.axis_size("dp") * lax.axis_size("tm") * lax.axis_size("space")
    partial = earlier_part(pair, corner, packed_second, partial)
    args = [
        *partner, packed_second, partial, *(mids[frame] for frame in range(frame_count)),
        slope, hidden_t, latent_t, predicted, student_out,
    ]
    teacher, mine, yours = call(
        functools.partial(last_body, columns, token_total),
        [rows_of(frame_count), shape(channels, channels, F32), square],
        [VMEM] * len(args), [VMEM] * 3,
        [pltpu.VMEM((tokens, channels), BF16)],
        12 * tokens * unit, 8 * tokens * channels, *args,
    )
    grad_in, grad_out = sum_everywhere(mine, yours)
    return (teacher.reshape(latent.shape), grad_in, grad_out)


def solution(mesh):
    return jax.shard_map(
        shards,
        mesh=mesh,
        in_specs=(
            P("dp", "tm", "space", None, None),
            P(),
            P(),
            P(),
            P(),
            P(),
            P(),
            P(),
            P(),
            P(),
            P(),
            P(),
        ),
        out_specs=(P("dp", "tm", "space", None, None), P(), P()),
        check_vma=False,
    )
```

```python
import functools

import jax
import jax.numpy as jnp
from jax import lax
from jax.experimental import pallas as pl
from jax.experimental.pallas import tpu as pltpu
from jax.sharding import PartitionSpec as P


F32 = jnp.float32
BF16 = jnp.bfloat16
VMEM = pl.BlockSpec(memory_space=pltpu.VMEM)
HBM = pl.BlockSpec(memory_space=pltpu.HBM)
LIMIT = 20 << 20


def xor_permute(value, axis, mask):
    count = lax.axis_size(axis)
    return lax.ppermute(value, axis, [(i, i ^ mask) for i in range(count)])


def gather_chips(block):
    mask = lax.axis_size("space") // 2
    blocks = [block]
    while mask > 1:
        blocks = blocks + [xor_permute(b, "space", mask) for b in blocks]
        mask //= 2
    return blocks[1:]


def across_pairs():
    pairs = []
    for low in range(1, lax.axis_size("space") - 1, 2):
        pairs += [(low, low + 1), (low + 1, low)]
    return pairs


def across_permute(value):
    clips, count = lax.axis_size("dp"), lax.axis_size("space")
    rows = dict(across_pairs())
    pairs = []
    for clip in range(clips):
        for place in range(count):
            other = (clip, rows[place]) if place in rows else (clip ^ 1, place)
            if other[0] < clips:
                pairs.append((clip * count + place, other[0] * count + other[1]))
    return lax.ppermute(value, ("dp", "space"), pairs)


def frame_pairings(value):
    blocks, count = lax.axis_size("tm"), lax.axis_size("space")
    results = []
    for first in range(2):
        pairs = []
        for block in range(blocks):
            other = ((block - first) ^ 1) + first
            for place in range(count):
                inside = 0 <= other < blocks
                target = other * count + place if inside else block * count + (place ^ 1)
                pairs.append((block * count + place, target))
        results.append(lax.ppermute(value, ("tm", "space"), pairs))
    return results


def across_next_frames(value):
    count = lax.axis_size("space")
    pairs = [
        (block * count + source, (block + 1) * count + target)
        for block in range(lax.axis_size("tm") - 1)
        for source, target in across_pairs()
    ]
    return lax.ppermute(value, ("tm", "space"), pairs)


def take_rows(value, index, rows):
    return lax.dynamic_slice_in_dim(value, index * rows, rows, axis=0)


def plane_permute(value, mask, dp_count):
    chips = lax.axis_size("space") // 2
    pairs = []
    for member in range(dp_count * chips):
        other = member ^ mask
        for core in range(2):
            source = (member // chips * chips + member % chips) * 2 + core
            target = (other // chips * chips + other % chips) * 2 + core
            pairs.append((source, target))
    return lax.ppermute(value, ("dp", "space"), pairs)


def span_permute(value, mask):
    return xor_permute(value, "tm", mask)


def sum_everywhere(mine, yours):
    odd = is_odd()
    dp_count, tm_count, space_count = (lax.axis_size(a) for a in ("dp", "tm", "space"))
    mine = mine + xor_permute(yours, "space", 1).astype(F32)
    members = dp_count * space_count // 2
    member = lax.axis_index("dp") * (space_count // 2) + lax.axis_index("space") // 2
    rows = mine.shape[0] // members
    sent = mine.astype(BF16)
    arrived = [
        plane_permute(take_rows(sent, member ^ mask, rows), mask, dp_count)
        for mask in range(1, members)
    ]
    chunk = take_rows(mine, member, rows)
    for piece in arrived:
        chunk = chunk + piece.astype(F32)
    chunk = chunk.astype(BF16)
    pieces = [chunk] + [span_permute(chunk, mask) for mask in range(1, tm_count)]
    pieces = [piece.astype(F32) for piece in pieces]
    while len(pieces) > 1:
        pieces = [pieces[i] + pieces[i + 1] for i in range(0, len(pieces), 2)]
    chunk = pieces[0].astype(BF16)
    whole = jnp.zeros(mine.shape, BF16)
    whole = lax.dynamic_update_slice_in_dim(whole, chunk, member * rows, axis=0)
    for mask in range(1, members):
        whole = lax.dynamic_update_slice_in_dim(
            whole, plane_permute(chunk, mask, dp_count), (member ^ mask) * rows, axis=0
        )
    other = xor_permute(whole, "space", 1)
    return (
        jnp.where(odd, other, whole).astype(F32),
        jnp.where(odd, whole, other).astype(F32),
    )


def root_norm(values, gain):
    return values * lax.rsqrt(jnp.mean(values * values, axis=-1, keepdims=True) + 1e-06) * gain


def silu(values):
    return values * jax.nn.sigmoid(values)


def dot(left, right):
    return jnp.dot(left, right, preferred_element_type=F32)


def call(body, outs, specs, out_specs, scratch, flops, moved, *args):
    return pl.pallas_call(
        body,
        out_shape=outs,
        in_specs=specs,
        out_specs=out_specs,
        scratch_shapes=scratch,
        compiler_params=pltpu.CompilerParams(vmem_limit_bytes=LIMIT),
        cost_estimate=pl.CostEstimate(
            flops=int(flops), bytes_accessed=int(moved), transcendentals=0
        ),
    )(*(
        pltpu.with_memory_space_constraint(arg, pltpu.HBM) if spec is HBM else arg
        for arg, spec in zip(args, specs, strict=True)
    ))


def shape(rows, columns, dtype):
    return jax.ShapeDtypeStruct((rows, columns), dtype)


def is_odd():
    return lax.rem(lax.axis_index("space"), 2) == 1


def has_across():
    place = lax.axis_index("space")
    return jnp.logical_and(place > 0, place < lax.axis_size("space") - 1)


def choose_frames(pair, here):
    block = lax.axis_index("tm")
    low, high = pair[0][here], pair[1][here]
    chosen = jnp.where(lax.rem(block, 2) == 1, low, high)
    return jnp.where(block > 0, chosen, jnp.zeros_like(chosen))


def edge_rows(values, columns, odd):
    first, last = values[:columns], values[values.shape[0] - columns :]
    return jnp.where(odd, first, last), jnp.where(odd, last, first)


def norm_body(latent_hbm, gain_hbm, latent, normed, *refs):
    frame_count, per_frame = latent_hbm.shape[:2]
    frames, gain, sems = refs[:frame_count], refs[-2], refs[-1]
    gain_copy = pltpu.make_async_copy(gain_hbm, gain, sems.at[frame_count])
    gain_copy.start()
    copies = {}
    for frame in range(frame_count - 1, -1, -1):
        here = pl.ds(frame * per_frame, per_frame)
        copies[frame] = pltpu.make_async_copy(latent_hbm.at[frame], latent.at[here], sems.at[frame])
        copies[frame].start()
    gain_copy.wait()
    for frame in range(frame_count - 1, -1, -1):
        here = pl.ds(frame * per_frame, per_frame)
        copies[frame].wait()
        wide = latent[here].astype(F32)
        result = root_norm(wide, gain[...].reshape(1, -1)).astype(BF16)
        normed[here] = result
        frames[frame][...] = result


def prepare_body(
    latent, normed, partner, query_hbm, key_hbm, value_hbm, out_hbm, in_hbm, back_hbm, first_hbm, second_hbm,
    w_both, w_out, s_out, first, second, slope, hidden_t, latent_t, predicted,
    queries, own_both, partner_both, w_query, s_in, sems,
):
    channels = latent.shape[1]
    early = [
        pltpu.make_async_copy(query_hbm, w_query, sems.at[2]),
        pltpu.make_async_copy(key_hbm, w_both.at[:, pl.ds(0, channels)], sems.at[3]),
        pltpu.make_async_copy(value_hbm, w_both.at[:, pl.ds(channels, channels)], sems.at[4]),
        pltpu.make_async_copy(in_hbm, s_in, sems.at[0]),
        pltpu.make_async_copy(back_hbm, s_out, sems.at[1]),
    ]
    rest = [pltpu.make_async_copy(out_hbm, w_out, sems.at[5])]
    for at, (taps, packed) in enumerate(((first_hbm, first), (second_hbm, second))):
        for t in range(3):
            for r in range(3):
                for c in range(3):
                    row = (3 * t + r) * channels
                    block = packed.at[pl.ds(row, channels), pl.ds(c * channels, channels)]
                    rest.append(
                        pltpu.make_async_copy(taps.at[t, r, c], block, sems.at[6 + 3 * at + t])
                    )
    for copy in early + rest:
        copy.start()
    tokens = latent[...]
    latent_t[...] = tokens.T
    early[0].wait()
    queries[...] = dot(normed[...], w_query[...]).astype(BF16)
    early[1].wait()
    early[2].wait()
    own_both[...] = dot(normed[...], w_both[...]).astype(BF16)
    partner_both[...] = dot(partner[...], w_both[...]).astype(BF16)
    early[3].wait()
    before = dot(tokens, s_in[...])
    hidden = silu(before).astype(BF16)
    logistic = jax.nn.sigmoid(before)
    slope[...] = logistic * (1.0 + before * (1.0 - logistic))
    hidden_t[...] = hidden.T
    early[4].wait()
    predicted[...] = tokens.astype(F32) + dot(hidden, s_out[...])
    for copy in rest:
        copy.wait()


def attend_body(frame, remote, columns, kept, *refs):
    blocks, refs = refs[:remote], refs[remote:]
    latent, queries, own_both, partner_both, w_both, w_out, gain = refs[:7]
    others, (act, mid, on, off) = refs[7 : 7 + kept], refs[7 + kept :]
    channels = w_out.shape[0]
    per_frame = mid.shape[0]
    odd = is_odd()
    for target, other in zip((on, off, act), others):
        rows = other.shape[0]
        target[pl.ds(target.shape[0] - rows, rows)] = other[...]
    here = pl.ds(frame * per_frame, per_frame)
    far = dot(jnp.concatenate([block[...] for block in blocks], axis=0), w_both[...]).astype(BF16)
    parts = [own_both[here], partner_both[here], far]
    keys = jnp.concatenate([part[:, :channels] for part in parts], axis=0)
    values = jnp.concatenate([part[:, channels:] for part in parts], axis=0)
    scores = lax.dot_general(
        queries[here], keys, (((1,), (1,)), ((), ())), preferred_element_type=F32
    ) * channels ** (-0.5)
    expos = jnp.exp(scores - jnp.max(scores, axis=-1, keepdims=True))
    totals = jnp.sum(expos, axis=-1, keepdims=True)
    mixed = (dot(expos.astype(BF16), values) / totals).astype(BF16)
    middle = (latent[here].astype(F32) + dot(mixed, w_out[...])).astype(BF16)
    mid[...] = middle
    active = silu(root_norm(middle.astype(F32), gain[...].reshape(1, -1))).astype(BF16)
    act[pl.ds(0, per_frame)] = active
    edge = pl.ds(0, columns)
    on[edge], off[edge] = edge_rows(active, columns, odd)


def stack_rows(columns, odd, own, on, off, stacked, at):
    per_frame, channels = own.shape
    base = at * per_frame
    split = per_frame - columns
    stacked[pl.ds(base, columns), 0:channels] = jnp.where(odd, on, off)
    stacked[pl.ds(base + columns, split), 0:channels] = own[:split]
    stacked[pl.ds(base, per_frame), channels : 2 * channels] = own
    stacked[pl.ds(base, split), 2 * channels :] = own[columns:]
    stacked[pl.ds(base + split, columns), 2 * channels :] = jnp.where(odd, off, on)


def taps_sum(sources, frame, stacked, packed, per_frame, total):
    at = [i for i, source in enumerate(sources) if 0 <= source - frame < 3]
    if not at:
        return total
    rows = [stacked[pl.ds(i * per_frame, per_frame)] for i in at]
    depth = stacked.shape[1]
    taps = packed[pl.ds((sources[at[0]] - frame) * depth, len(at) * depth)]
    term = dot(jnp.concatenate(rows, axis=1), taps)
    return term if total is None else total + term


def shift_columns(total, columns):
    rows, channels = total.shape[0], total.shape[1] // 3
    column = lax.broadcasted_iota(jnp.int32, (rows, channels), 0) % columns
    before = pltpu.roll(total[:, :channels], 1, 0)
    after = pltpu.roll(total[:, 2 * channels :], rows - 1, 0)
    return (
        total[:, channels : 2 * channels]
        + jnp.where(column == 0, 0.0, before)
        + jnp.where(column == columns - 1, 0.0, after)
    )


def own_body(groups, columns, *refs):
    odd = is_odd()
    far = has_across()
    off, on, packed, partial, stacked = refs[-5:]
    frame_count = sum(groups)
    per_frame = partial.shape[0] // frame_count
    at = 0
    for own, frames in zip(refs[:-5], groups, strict=True):
        for frame in range(frames):
            edge = pl.ds(at * columns, columns)
            stack_rows(
                columns, odd, own[pl.ds(frame * per_frame, per_frame)], on[edge],
                jnp.where(far, off[edge], jnp.zeros_like(off[edge])), stacked, at,
            )
            at += 1
    sources = range(2, frame_count + 2)
    for frame in range(frame_count):
        total = taps_sum(sources, frame, stacked, packed, per_frame, None)
        partial[pl.ds(frame * per_frame, per_frame)] = total


def earlier_body(columns, low, high, off, packed, partial, total, stacked):
    odd = is_odd()
    per_frame = stacked.shape[0] // 2
    for frame in range(2):
        tail = choose_frames((low, high), pl.ds(frame * per_frame, per_frame))
        edge = off[pl.ds(frame * columns, columns)]
        stack_rows(columns, odd, tail, jnp.zeros_like(edge), edge, stacked, frame)
    for frame in range(total.shape[0] // per_frame):
        here = pl.ds(frame * per_frame, per_frame)
        total[here] = taps_sum((0, 1), frame, stacked, packed, per_frame, partial[here])


def partner_terms(columns, odd, pair, packed):
    per_frame = pair[0].shape[0] // 2
    channels = pair[0].shape[1]
    row = jnp.where(odd, 0, 2 * channels)
    edges = []
    for source in range(2):
        rows = choose_frames(pair, pl.ds(source * per_frame, per_frame))
        edges.append(edge_rows(rows, columns, jnp.logical_not(odd))[0])
    terms = []
    for frame in range(2):
        term = None
        for source in range(frame, 2):
            start = pl.multiple_of(3 * (source - frame) * channels + row, channels)
            part = dot(edges[source], packed[pl.ds(start, channels)])
            term = part if term is None else term + part
        zeros = jnp.zeros_like(term)
        pieces = [jnp.where(odd, term, zeros), jnp.where(odd, zeros, term)]
        if per_frame > 2 * columns:
            pieces.insert(1, jnp.zeros((per_frame - 2 * columns, term.shape[1]), F32))
        terms.append(jnp.concatenate(pieces, axis=0))
    return terms


def first_body(
    columns, low, high, packed, changed, partial, gain, act, late, on, off, off_late
):
    odd = is_odd()
    terms = partner_terms(columns, odd, (low, high), packed)
    per_frame = low.shape[0] // 2
    frame_count = partial.shape[0] // per_frame
    for frame in range(frame_count - 1, -1, -1):
        here = pl.ds(frame * per_frame, per_frame)
        total = changed[here] + terms[frame] if frame < 2 else partial[here]
        total = shift_columns(total, columns)
        active = silu(root_norm(total, gain[...].reshape(1, -1))).astype(BF16)
        act[here] = active
        edge = pl.ds(frame * columns, columns)
        near, far = edge_rows(active, columns, odd)
        on[edge], off[edge] = near, far
        at = frame - (frame_count - 2)
        if at >= 0:
            late[pl.ds(at * per_frame, per_frame)] = active
            off_late[pl.ds(at * columns, columns)] = far


def last_body(columns, token_total, low, high, packed, changed, partial, *refs):
    slope, hidden_t, latent_t, predicted, s_out, teacher, mine, yours, signals = refs[-9:]
    mids = refs[:-9]
    odd = is_odd()
    terms = partner_terms(columns, odd, (low, high), packed)
    per_frame = low.shape[0] // 2
    frame_count = partial.shape[0] // per_frame
    for frame in range(frame_count - 1, -1, -1):
        here = pl.ds(frame * per_frame, per_frame)
        total = changed[here] + terms[frame] if frame < 2 else partial[here]
        total = shift_columns(total, columns)
        taught = (mids[frame][...].astype(F32) + total).astype(BF16)
        teacher[here] = taught
        error = predicted[here] - taught.astype(F32)
        signals[here] = (
            error * lax.rsqrt(error * error + 0.0625) * token_total ** (-0.5)
        ).astype(BF16)
    signal = signals[...]
    grad_out = dot(hidden_t[...], signal)
    back = lax.dot_general(
        signal, s_out[...], (((1,), (1,)), ((), ())), preferred_element_type=F32
    )
    back_pre = (back * slope[...]).astype(BF16)
    grad_in = dot(latent_t[...], back_pre)
    mine[...] = jnp.where(odd, grad_out, grad_in)
    yours[...] = jnp.where(odd, grad_in, grad_out).astype(BF16)


def shards(
    latent,
    attn_gain,
    w_query,
    w_key,
    w_value,
    w_out,
    conv_gain_first,
    conv_first,
    conv_gain_second,
    conv_second,
    student_in,
    student_out,
):
    frame_count, row_count, columns, channels = latent.shape[1:]
    per_frame = row_count * columns
    tokens = frame_count * per_frame
    early = frame_count - 2
    frames = latent.reshape(frame_count, per_frame, channels)
    unit = 2 * channels * channels
    square = shape(channels, channels, BF16)

    def rows_of(count):
        return shape(count * per_frame, channels, BF16)

    def edges_of(count):
        return shape(count * columns, channels, BF16)

    latent_rows, normed, *singles = call(
        norm_body,
        [rows_of(frame_count), rows_of(frame_count)] + [rows_of(1)] * frame_count,
        [HBM] * 2, [VMEM] * (2 + frame_count),
        [pltpu.VMEM((channels,), F32), pltpu.SemaphoreType.DMA((frame_count + 1,))],
        0, 4 * tokens * channels, frames, attn_gain,
    )
    order = list(range(frame_count - 1, -1, -1))
    gathered = {frame: gather_chips(singles[frame]) for frame in order}

    packed_shape = shape(9 * channels, 3 * channels, BF16)
    wide = shape(tokens, channels, F32)
    turned = shape(channels, tokens, BF16)
    both = shape(tokens, 2 * channels, BF16)
    weights = (w_query, w_key, w_value, w_out, student_in, student_out, conv_first, conv_second)
    (
        w_both, w_out, student_out, packed_first, packed_second,
        slope, hidden_t, latent_t, predicted, queries, own_both, partner_both,
    ) = call(
        prepare_body,
        [shape(channels, 2 * channels, BF16), square, square, packed_shape, packed_shape,
         wide, turned, turned, wide, rows_of(frame_count), both, both],
        [VMEM] * 3 + [HBM] * len(weights), [VMEM] * 12,
        [pltpu.VMEM((channels, channels), BF16)] * 2 + [pltpu.SemaphoreType.DMA((12,))],
        7 * tokens * unit, 60 * channels * channels * 2,
        latent_rows, normed, xor_permute(normed, "space", 1), *weights,
    )

    acts, mids, others = {}, {}, ()
    for turn, frame in enumerate(order):
        chips = gathered[frame]
        blocks = [*chips, *(xor_permute(block, "space", 1) for block in chips)]
        args = [
            *blocks, latent_rows, queries, own_both, partner_both, w_both, w_out,
            conv_gain_first, *others,
        ]
        ends = edges_of(turn + 1)
        acts[frame], mids[frame], on, off = call(
            functools.partial(attend_body, frame, len(blocks), columns, len(others)),
            [rows_of(2 if turn == 1 else 1), rows_of(1), ends, ends],
            [VMEM] * len(args), [VMEM] * 4, [],
            (4 + 2 * len(blocks)) * per_frame * unit, 4 * per_frame * channels, *args,
        )
        others = (on, off, acts[frame]) if turn == 0 else (on, off)
        if turn == 1:
            late, off_late = acts[frame], off

    def stacked(count):
        return pltpu.VMEM((count * per_frame, 3 * channels), BF16)

    def from_earlier(late, off):
        pair = frame_pairings(late)
        corner = across_next_frames(off)
        partner = [xor_permute(frames, "space", 1) for frames in pair]
        return pair, corner, partner

    def earlier_part(pair, corner, packed, partial):
        args = [*pair, corner, packed, partial]
        return call(
            functools.partial(earlier_body, columns),
            shape(2 * per_frame, 3 * channels, F32), [VMEM] * len(args), VMEM,
            [stacked(2)], 9 * tokens * unit, 8 * tokens * channels, *args,
        )

    def own_part(groups, on, off, packed):
        halo = [across_permute(off)]
        halo.append(xor_permute(on, "space", 1))
        args = [*(own for _, own in groups), *halo, packed]
        return call(
            functools.partial(own_body, [group[0] for group in groups], columns),
            shape(tokens, 3 * channels, F32), [VMEM] * len(args), VMEM,
            [stacked(frame_count)], 18 * tokens * unit, 8 * tokens * channels, *args,
        )

    pair, corner, partner = from_earlier(late, off_late)
    groups = [(1, acts[frame]) for frame in range(early)] + [(2, late)]
    partial = own_part(groups, on, off, packed_first)
    changed = earlier_part(pair, corner, packed_first, partial)
    args = [*partner, packed_first, changed, partial, conv_gain_second]
    act, late, on, off, off_late = call(
        functools.partial(first_body, columns),
        [rows_of(frame_count), rows_of(2), edges_of(frame_count), edges_of(frame_count), edges_of(2)],
        [VMEM] * len(args), [VMEM] * 5, [],
        9 * tokens * unit, 8 * tokens * channels, *args,
    )
    pair, corner, partner = from_earlier(late, off_late)
    partial = own_part([(frame_count, act)], on, off, packed_second)
    token_total = tokens * lax.axis_size("dp") * lax.axis_size("tm") * lax.axis_size("space")
    changed = earlier_part(pair, corner, packed_second, partial)
    args = [
        *partner, packed_second, changed, partial, *(mids[frame] for frame in range(frame_count)),
        slope, hidden_t, latent_t, predicted, student_out,
    ]
    teacher, mine, yours = call(
        functools.partial(last_body, columns, token_total),
        [rows_of(frame_count), shape(channels, channels, F32), square],
        [VMEM] * len(args), [VMEM] * 3,
        [pltpu.VMEM((tokens, channels), BF16)],
        12 * tokens * unit, 8 * tokens * channels, *args,
    )
    grad_in, grad_out = sum_everywhere(mine, yours)
    return (teacher.reshape(latent.shape), grad_in, grad_out)


def solution(mesh):
    return jax.shard_map(
        shards,
        mesh=mesh,
        in_specs=(
            P("dp", "tm", "space", None, None),
            P(),
            P(),
            P(),
            P(),
            P(),
            P(),
            P(),
            P(),
            P(),
            P(),
            P(),
        ),
        out_specs=(P("dp", "tm", "space", None, None), P(), P()),
        check_vma=False,
    )
```

```python
import functools

import jax
import jax.numpy as jnp
from jax import lax
from jax.experimental import pallas as pl
from jax.experimental.pallas import tpu as pltpu
from jax.sharding import PartitionSpec as P


F32 = jnp.float32
BF16 = jnp.bfloat16
VMEM = pl.BlockSpec(memory_space=pltpu.VMEM)
HBM = pl.BlockSpec(memory_space=pltpu.HBM)
LIMIT = 20 << 20


def xor_permute(value, axis, mask):
    count = lax.axis_size(axis)
    return lax.ppermute(value, axis, [(i, i ^ mask) for i in range(count)])


def gather_chips(block):
    mask = lax.axis_size("space") // 2
    blocks = [block]
    while mask > 1:
        blocks = blocks + [xor_permute(b, "space", mask) for b in blocks]
        mask //= 2
    return blocks[1:]


def across_pairs():
    pairs = []
    for low in range(1, lax.axis_size("space") - 1, 2):
        pairs += [(low, low + 1), (low + 1, low)]
    return pairs


def across_permute(value):
    clips, count = lax.axis_size("dp"), lax.axis_size("space")
    rows = dict(across_pairs())
    pairs = []
    for clip in range(clips):
        for place in range(count):
            other = (clip, rows[place]) if place in rows else (clip ^ 1, place)
            if other[0] < clips:
                pairs.append((clip * count + place, other[0] * count + other[1]))
    return lax.ppermute(value, ("dp", "space"), pairs)


def frame_pairings(value):
    blocks, count = lax.axis_size("tm"), lax.axis_size("space")
    results = []
    for first in range(2):
        pairs = []
        for block in range(blocks):
            other = ((block - first) ^ 1) + first
            for place in range(count):
                inside = 0 <= other < blocks
                target = other * count + place if inside else block * count + (place ^ 1)
                pairs.append((block * count + place, target))
        results.append(lax.ppermute(value, ("tm", "space"), pairs))
    return results


def across_next_frames(value):
    count = lax.axis_size("space")
    pairs = [
        (block * count + source, (block + 1) * count + target)
        for block in range(lax.axis_size("tm") - 1)
        for source, target in across_pairs()
    ]
    return lax.ppermute(value, ("tm", "space"), pairs)


def take_rows(value, index, rows):
    return lax.dynamic_slice_in_dim(value, index * rows, rows, axis=0)


def plane_permute(value, mask, dp_count):
    chips = lax.axis_size("space") // 2
    pairs = []
    for member in range(dp_count * chips):
        other = member ^ mask
        for core in range(2):
            source = (member // chips * chips + member % chips) * 2 + core
            target = (other // chips * chips + other % chips) * 2 + core
            pairs.append((source, target))
    return lax.ppermute(value, ("dp", "space"), pairs)


def span_permute(value, mask):
    return xor_permute(value, "tm", mask)


def sum_everywhere(mine, yours):
    odd = is_odd()
    dp_count, tm_count, space_count = (lax.axis_size(a) for a in ("dp", "tm", "space"))
    mine = mine + xor_permute(yours, "space", 1).astype(F32)
    members = dp_count * space_count // 2
    member = lax.axis_index("dp") * (space_count // 2) + lax.axis_index("space") // 2
    rows = mine.shape[0] // members
    sent = mine.astype(BF16)
    arrived = [
        plane_permute(take_rows(sent, member ^ mask, rows), mask, dp_count)
        for mask in range(1, members)
    ]
    chunk = take_rows(mine, member, rows)
    for piece in arrived:
        chunk = chunk + piece.astype(F32)
    chunk = chunk.astype(BF16)
    pieces = [chunk] + [span_permute(chunk, mask) for mask in range(1, tm_count)]
    pieces = [piece.astype(F32) for piece in pieces]
    while len(pieces) > 1:
        pieces = [pieces[i] + pieces[i + 1] for i in range(0, len(pieces), 2)]
    chunk = pieces[0].astype(BF16)
    whole = jnp.zeros(mine.shape, BF16)
    whole = lax.dynamic_update_slice_in_dim(whole, chunk, member * rows, axis=0)
    for mask in range(1, members):
        whole = lax.dynamic_update_slice_in_dim(
            whole, plane_permute(chunk, mask, dp_count), (member ^ mask) * rows, axis=0
        )
    other = xor_permute(whole, "space", 1)
    return (
        jnp.where(odd, other, whole).astype(F32),
        jnp.where(odd, whole, other).astype(F32),
    )


def root_norm(values, gain):
    return values * lax.rsqrt(jnp.mean(values * values, axis=-1, keepdims=True) + 1e-06) * gain


def silu(values):
    return values * jax.nn.sigmoid(values)


def dot(left, right):
    return jnp.dot(left, right, preferred_element_type=F32)


def call(body, outs, specs, out_specs, scratch, flops, moved, *args):
    return pl.pallas_call(
        body,
        out_shape=outs,
        in_specs=specs,
        out_specs=out_specs,
        scratch_shapes=scratch,
        compiler_params=pltpu.CompilerParams(vmem_limit_bytes=LIMIT),
        cost_estimate=pl.CostEstimate(
            flops=int(flops), bytes_accessed=int(moved), transcendentals=0
        ),
    )(*(
        pltpu.with_memory_space_constraint(arg, pltpu.HBM) if spec is HBM else arg
        for arg, spec in zip(args, specs, strict=True)
    ))


def shape(rows, columns, dtype):
    return jax.ShapeDtypeStruct((rows, columns), dtype)


def is_odd():
    return lax.rem(lax.axis_index("space"), 2) == 1


def has_across():
    place = lax.axis_index("space")
    return jnp.logical_and(place > 0, place < lax.axis_size("space") - 1)


def choose_frames(pair, here):
    block = lax.axis_index("tm")
    low, high = pair[0][here], pair[1][here]
    chosen = jnp.where(lax.rem(block, 2) == 1, low, high)
    return jnp.where(block > 0, chosen, jnp.zeros_like(chosen))


def edge_rows(values, columns, odd):
    first, last = values[:columns], values[values.shape[0] - columns :]
    return jnp.where(odd, first, last), jnp.where(odd, last, first)


def norm_body(latent_hbm, gain_hbm, latent, normed, *refs):
    frame_count, per_frame = latent_hbm.shape[:2]
    frames, gain, sems = refs[:frame_count], refs[-2], refs[-1]
    gain_copy = pltpu.make_async_copy(gain_hbm, gain, sems.at[frame_count])
    gain_copy.start()
    copies = {}
    for frame in range(frame_count - 1, -1, -1):
        here = pl.ds(frame * per_frame, per_frame)
        copies[frame] = pltpu.make_async_copy(latent_hbm.at[frame], latent.at[here], sems.at[frame])
        copies[frame].start()
    gain_copy.wait()
    for frame in range(frame_count - 1, -1, -1):
        here = pl.ds(frame * per_frame, per_frame)
        copies[frame].wait()
        wide = latent[here].astype(F32)
        result = root_norm(wide, gain[...].reshape(1, -1)).astype(BF16)
        normed[here] = result
        frames[frame][...] = result


def tap_copies(taps, packed, sem):
    channels = taps.shape[3]
    return [
        pltpu.make_async_copy(
            taps.at[t, r, c],
            packed.at[pl.ds((3 * t + r) * channels, channels), pl.ds(c * channels, channels)],
            sem,
        )
        for t in range(3)
        for r in range(3)
        for c in range(3)
    ]


def prepare_body(
    latent, normed, partner, query_hbm, key_hbm, value_hbm, out_hbm, in_hbm, back_hbm, first_hbm,
    w_both, w_out, s_out, first, slope, hidden_t, latent_t, predicted,
    queries, own_both, partner_both, w_query, s_in, sems,
):
    channels = latent.shape[1]
    early = [
        pltpu.make_async_copy(query_hbm, w_query, sems.at[2]),
        pltpu.make_async_copy(key_hbm, w_both.at[:, pl.ds(0, channels)], sems.at[3]),
        pltpu.make_async_copy(value_hbm, w_both.at[:, pl.ds(channels, channels)], sems.at[4]),
        pltpu.make_async_copy(in_hbm, s_in, sems.at[0]),
        pltpu.make_async_copy(back_hbm, s_out, sems.at[1]),
    ]
    rest = [pltpu.make_async_copy(out_hbm, w_out, sems.at[5])]
    rest += tap_copies(first_hbm, first, sems.at[6])
    for copy in early + rest:
        copy.start()
    tokens = latent[...]
    latent_t[...] = tokens.T
    early[0].wait()
    queries[...] = dot(normed[...], w_query[...]).astype(BF16)
    early[1].wait()
    early[2].wait()
    own_both[...] = dot(normed[...], w_both[...]).astype(BF16)
    partner_both[...] = dot(partner[...], w_both[...]).astype(BF16)
    early[3].wait()
    before = dot(tokens, s_in[...])
    hidden = silu(before).astype(BF16)
    logistic = jax.nn.sigmoid(before)
    slope[...] = logistic * (1.0 + before * (1.0 - logistic))
    hidden_t[...] = hidden.T
    early[4].wait()
    predicted[...] = tokens.astype(F32) + dot(hidden, s_out[...])
    for copy in rest:
        copy.wait()


def attend_body(frame, remote, columns, kept, *refs):
    blocks, refs = refs[:remote], refs[remote:]
    latent, queries, own_both, partner_both, w_both, w_out, gain = refs[:7]
    others, (act, mid, on, off) = refs[7 : 7 + kept], refs[7 + kept :]
    channels = w_out.shape[0]
    per_frame = mid.shape[0]
    odd = is_odd()
    for target, other in zip((on, off, act), others):
        rows = other.shape[0]
        target[pl.ds(target.shape[0] - rows, rows)] = other[...]
    here = pl.ds(frame * per_frame, per_frame)
    far = dot(jnp.concatenate([block[...] for block in blocks], axis=0), w_both[...]).astype(BF16)
    parts = [own_both[here], partner_both[here], far]
    keys = jnp.concatenate([part[:, :channels] for part in parts], axis=0)
    values = jnp.concatenate([part[:, channels:] for part in parts], axis=0)
    scores = lax.dot_general(
        queries[here], keys, (((1,), (1,)), ((), ())), preferred_element_type=F32
    ) * channels ** (-0.5)
    expos = jnp.exp(scores - jnp.max(scores, axis=-1, keepdims=True))
    totals = jnp.sum(expos, axis=-1, keepdims=True)
    mixed = (dot(expos.astype(BF16), values) / totals).astype(BF16)
    middle = (latent[here].astype(F32) + dot(mixed, w_out[...])).astype(BF16)
    mid[...] = middle
    active = silu(root_norm(middle.astype(F32), gain[...].reshape(1, -1))).astype(BF16)
    act[pl.ds(0, per_frame)] = active
    edge = pl.ds(0, columns)
    on[edge], off[edge] = edge_rows(active, columns, odd)


def stack_rows(columns, odd, own, on, off, stacked, at):
    per_frame, channels = own.shape
    base = at * per_frame
    split = per_frame - columns
    stacked[pl.ds(base, columns), 0:channels] = jnp.where(odd, on, off)
    stacked[pl.ds(base + columns, split), 0:channels] = own[:split]
    stacked[pl.ds(base, per_frame), channels : 2 * channels] = own
    stacked[pl.ds(base, split), 2 * channels :] = own[columns:]
    stacked[pl.ds(base + split, columns), 2 * channels :] = jnp.where(odd, off, on)


def taps_sum(sources, frame, stacked, packed, per_frame, total):
    at = [i for i, source in enumerate(sources) if 0 <= source - frame < 3]
    if not at:
        return total
    rows = [stacked[pl.ds(i * per_frame, per_frame)] for i in at]
    depth = stacked.shape[1]
    taps = packed[pl.ds((sources[at[0]] - frame) * depth, len(at) * depth)]
    term = dot(jnp.concatenate(rows, axis=1), taps)
    return term if total is None else total + term


def shift_columns(total, columns):
    rows, channels = total.shape[0], total.shape[1] // 3
    column = lax.broadcasted_iota(jnp.int32, (rows, channels), 0) % columns
    before = pltpu.roll(total[:, :channels], 1, 0)
    after = pltpu.roll(total[:, 2 * channels :], rows - 1, 0)
    return (
        total[:, channels : 2 * channels]
        + jnp.where(column == 0, 0.0, before)
        + jnp.where(column == columns - 1, 0.0, after)
    )


def own_body(groups, columns, fetch, *refs):
    odd = is_odd()
    far = has_across()
    own_refs, refs = refs[: len(groups)], refs[len(groups) :]
    copies = []
    if fetch:
        off, on, packed, taps, partial, fetched, stacked, sem = refs
        copies = tap_copies(taps, fetched, sem.at[0])
    else:
        off, on, packed, partial, stacked = refs
    for copy in copies:
        copy.start()
    frame_count = sum(groups)
    per_frame = partial.shape[0] // frame_count
    at = 0
    for own, frames in zip(own_refs, groups, strict=True):
        for frame in range(frames):
            edge = pl.ds(at * columns, columns)
            stack_rows(
                columns, odd, own[pl.ds(frame * per_frame, per_frame)], on[edge],
                jnp.where(far, off[edge], jnp.zeros_like(off[edge])), stacked, at,
            )
            at += 1
    sources = range(2, frame_count + 2)
    for frame in range(frame_count):
        total = taps_sum(sources, frame, stacked, packed, per_frame, None)
        partial[pl.ds(frame * per_frame, per_frame)] = total
    for copy in copies:
        copy.wait()


def earlier_body(columns, low, high, off, packed, partial, total, stacked):
    odd = is_odd()
    per_frame = stacked.shape[0] // 2
    for frame in range(2):
        tail = choose_frames((low, high), pl.ds(frame * per_frame, per_frame))
        edge = off[pl.ds(frame * columns, columns)]
        stack_rows(columns, odd, tail, jnp.zeros_like(edge), edge, stacked, frame)
    for frame in range(total.shape[0] // per_frame):
        here = pl.ds(frame * per_frame, per_frame)
        total[here] = taps_sum((0, 1), frame, stacked, packed, per_frame, partial[here])


def partner_terms(columns, odd, pair, packed):
    per_frame = pair[0].shape[0] // 2
    channels = pair[0].shape[1]
    row = jnp.where(odd, 0, 2 * channels)
    edges = []
    for source in range(2):
        rows = choose_frames(pair, pl.ds(source * per_frame, per_frame))
        edges.append(edge_rows(rows, columns, jnp.logical_not(odd))[0])
    terms = []
    for frame in range(2):
        term = None
        for source in range(frame, 2):
            start = pl.multiple_of(3 * (source - frame) * channels + row, channels)
            part = dot(edges[source], packed[pl.ds(start, channels)])
            term = part if term is None else term + part
        zeros = jnp.zeros_like(term)
        pieces = [jnp.where(odd, term, zeros), jnp.where(odd, zeros, term)]
        if per_frame > 2 * columns:
            pieces.insert(1, jnp.zeros((per_frame - 2 * columns, term.shape[1]), F32))
        terms.append(jnp.concatenate(pieces, axis=0))
    return terms


def first_body(
    columns, low, high, packed, changed, partial, gain, act, late, on, off, off_late
):
    odd = is_odd()
    terms = partner_terms(columns, odd, (low, high), packed)
    per_frame = low.shape[0] // 2
    frame_count = partial.shape[0] // per_frame
    for frame in range(frame_count - 1, -1, -1):
        here = pl.ds(frame * per_frame, per_frame)
        total = changed[here] + terms[frame] if frame < 2 else partial[here]
        total = shift_columns(total, columns)
        active = silu(root_norm(total, gain[...].reshape(1, -1))).astype(BF16)
        act[here] = active
        edge = pl.ds(frame * columns, columns)
        near, far = edge_rows(active, columns, odd)
        on[edge], off[edge] = near, far
        at = frame - (frame_count - 2)
        if at >= 0:
            late[pl.ds(at * per_frame, per_frame)] = active
            off_late[pl.ds(at * columns, columns)] = far


def last_body(columns, token_total, low, high, packed, changed, partial, *refs):
    slope, hidden_t, latent_t, predicted, s_out, teacher, mine, yours, signals = refs[-9:]
    mids = refs[:-9]
    odd = is_odd()
    terms = partner_terms(columns, odd, (low, high), packed)
    per_frame = low.shape[0] // 2
    frame_count = partial.shape[0] // per_frame
    for frame in range(frame_count - 1, -1, -1):
        here = pl.ds(frame * per_frame, per_frame)
        total = changed[here] + terms[frame] if frame < 2 else partial[here]
        total = shift_columns(total, columns)
        taught = (mids[frame][...].astype(F32) + total).astype(BF16)
        teacher[here] = taught
        error = predicted[here] - taught.astype(F32)
        signals[here] = (
            error * lax.rsqrt(error * error + 0.0625) * token_total ** (-0.5)
        ).astype(BF16)
    signal = signals[...]
    grad_out = dot(hidden_t[...], signal)
    back = lax.dot_general(
        signal, s_out[...], (((1,), (1,)), ((), ())), preferred_element_type=F32
    )
    back_pre = (back * slope[...]).astype(BF16)
    grad_in = dot(latent_t[...], back_pre)
    mine[...] = jnp.where(odd, grad_out, grad_in)
    yours[...] = jnp.where(odd, grad_in, grad_out).astype(BF16)


def shards(
    latent,
    attn_gain,
    w_query,
    w_key,
    w_value,
    w_out,
    conv_gain_first,
    conv_first,
    conv_gain_second,
    conv_second,
    student_in,
    student_out,
):
    frame_count, row_count, columns, channels = latent.shape[1:]
    per_frame = row_count * columns
    tokens = frame_count * per_frame
    early = frame_count - 2
    frames = latent.reshape(frame_count, per_frame, channels)
    unit = 2 * channels * channels
    square = shape(channels, channels, BF16)

    def rows_of(count):
        return shape(count * per_frame, channels, BF16)

    def edges_of(count):
        return shape(count * columns, channels, BF16)

    latent_rows, normed, *singles = call(
        norm_body,
        [rows_of(frame_count), rows_of(frame_count)] + [rows_of(1)] * frame_count,
        [HBM] * 2, [VMEM] * (2 + frame_count),
        [pltpu.VMEM((channels,), F32), pltpu.SemaphoreType.DMA((frame_count + 1,))],
        0, 4 * tokens * channels, frames, attn_gain,
    )
    order = list(range(frame_count - 1, -1, -1))
    gathered = {frame: gather_chips(singles[frame]) for frame in order}

    packed_shape = shape(9 * channels, 3 * channels, BF16)
    wide = shape(tokens, channels, F32)
    turned = shape(channels, tokens, BF16)
    both = shape(tokens, 2 * channels, BF16)
    weights = (w_query, w_key, w_value, w_out, student_in, student_out, conv_first)
    (
        w_both, w_out, student_out, packed_first,
        slope, hidden_t, latent_t, predicted, queries, own_both, partner_both,
    ) = call(
        prepare_body,
        [shape(channels, 2 * channels, BF16), square, square, packed_shape,
         wide, turned, turned, wide, rows_of(frame_count), both, both],
        [VMEM] * 3 + [HBM] * len(weights), [VMEM] * 11,
        [pltpu.VMEM((channels, channels), BF16)] * 2 + [pltpu.SemaphoreType.DMA((7,))],
        7 * tokens * unit, 60 * channels * channels * 2,
        latent_rows, normed, xor_permute(normed, "space", 1), *weights,
    )

    acts, mids, others = {}, {}, ()
    for turn, frame in enumerate(order):
        chips = gathered[frame]
        blocks = [*chips, *(xor_permute(block, "space", 1) for block in chips)]
        args = [
            *blocks, latent_rows, queries, own_both, partner_both, w_both, w_out,
            conv_gain_first, *others,
        ]
        ends = edges_of(turn + 1)
        acts[frame], mids[frame], on, off = call(
            functools.partial(attend_body, frame, len(blocks), columns, len(others)),
            [rows_of(2 if turn == 1 else 1), rows_of(1), ends, ends],
            [VMEM] * len(args), [VMEM] * 4, [],
            (4 + 2 * len(blocks)) * per_frame * unit, 4 * per_frame * channels, *args,
        )
        others = (on, off, acts[frame]) if turn == 0 else (on, off)
        if turn == 1:
            late, off_late = acts[frame], off

    def stacked(count):
        return pltpu.VMEM((count * per_frame, 3 * channels), BF16)

    def from_earlier(late, off):
        pair = frame_pairings(late)
        corner = across_next_frames(off)
        partner = [xor_permute(frames, "space", 1) for frames in pair]
        return pair, corner, partner

    def earlier_part(pair, corner, packed, partial):
        args = [*pair, corner, packed, partial]
        return call(
            functools.partial(earlier_body, columns),
            shape(2 * per_frame, 3 * channels, F32), [VMEM] * len(args), VMEM,
            [stacked(2)], 9 * tokens * unit, 8 * tokens * channels, *args,
        )

    def own_part(groups, on, off, packed, *taps):
        halo = [across_permute(off)]
        halo.append(xor_permute(on, "space", 1))
        args = [*(own for _, own in groups), *halo, packed]
        outs = [shape(tokens, 3 * channels, F32)] + [packed_shape] * len(taps)
        return call(
            functools.partial(own_body, [group[0] for group in groups], columns, bool(taps)),
            outs, [VMEM] * len(args) + [HBM] * len(taps), [VMEM] * len(outs),
            [stacked(frame_count)] + [pltpu.SemaphoreType.DMA((1,))] * len(taps),
            18 * tokens * unit, 8 * tokens * channels, *args, *taps,
        )

    pair, corner, partner = from_earlier(late, off_late)
    groups = [(1, acts[frame]) for frame in range(early)] + [(2, late)]
    partial, packed_second = own_part(groups, on, off, packed_first, conv_second)
    changed = earlier_part(pair, corner, packed_first, partial)
    args = [*partner, packed_first, changed, partial, conv_gain_second]
    act, late, on, off, off_late = call(
        functools.partial(first_body, columns),
        [rows_of(frame_count), rows_of(2), edges_of(frame_count), edges_of(frame_count), edges_of(2)],
        [VMEM] * len(args), [VMEM] * 5, [],
        9 * tokens * unit, 8 * tokens * channels, *args,
    )
    pair, corner, partner = from_earlier(late, off_late)
    (partial,) = own_part([(frame_count, act)], on, off, packed_second)
    token_total = tokens * lax.axis_size("dp") * lax.axis_size("tm") * lax.axis_size("space")
    changed = earlier_part(pair, corner, packed_second, partial)
    args = [
        *partner, packed_second, changed, partial, *(mids[frame] for frame in range(frame_count)),
        slope, hidden_t, latent_t, predicted, student_out,
    ]
    teacher, mine, yours = call(
        functools.partial(last_body, columns, token_total),
        [rows_of(frame_count), shape(channels, channels, F32), square],
        [VMEM] * len(args), [VMEM] * 3,
        [pltpu.VMEM((tokens, channels), BF16)],
        12 * tokens * unit, 8 * tokens * channels, *args,
    )
    grad_in, grad_out = sum_everywhere(mine, yours)
    return (teacher.reshape(latent.shape), grad_in, grad_out)


def solution(mesh):
    return jax.shard_map(
        shards,
        mesh=mesh,
        in_specs=(
            P("dp", "tm", "space", None, None),
            P(),
            P(),
            P(),
            P(),
            P(),
            P(),
            P(),
            P(),
            P(),
            P(),
            P(),
        ),
        out_specs=(P("dp", "tm", "space", None, None), P(), P()),
        check_vma=False,
    )
```
